128 devices in a mesh: gx: 16 (over x, y), gy: 8 (over z, core).
Axes of the slice: x: 4, y: 4, z: 4, core: 2. Of those that a mesh axis runs over, the one named last changes fastest.
Arguments:
- near_null: float32 [768, 64, 2048], P('gx', 'gy')
- a_blocks: bfloat16 [768, 64, 4, 4096], P('gx', 'gy'), may hold values from -0.375 to 0.375
- inv_diag: float32 [768, 64, 64], P('gx', 'gy'), may hold values from 0.5 to 2
- root_map: int32 [768, 64], P('gx', 'gy'), may hold values from 0 to 49151, as said below
- neighbours: int32 [768, 64, 4], P('gx', 'gy'), may hold values from 0 to 49151, as said below
Outputs:
- prolong: float32 [768, 64, 2048], P('gx', 'gy')
The draws below stay inside these ranges and needn't reach their ends.
Inputs may be any that keep to these rules, and one draw needn't show every extreme that they name: `root_map`: each element's root lies within 2 elements of it along both grid dimensions, and every root is its own root. `neighbours`: entry 0 of each element's list is the element itself; the other 3 entries are distinct other elements within 2 elements of it along both grid dimensions.
All inputs are finite; a program needn't handle non-finite values.
Results may differ from the reference program's by a relative error of at most 0.0017.
Values may be sent and summed in bfloat16 or wider, within the bound.
A program may use at most 384 MiB of HBM per device.

```python
import math
import jax
import jax.numpy as jnp
import numpy as np
from jax import lax

ORDER = 64
MODES = 32
COUPLINGS = 4
NXE = 768
NYE = 64


def draw_near_null(key, part):
    key_base = jax.random.fold_in(key, 0)
    values = jax.random.normal(key_base, (NXE, NYE, ORDER, MODES), jnp.float32)
    return values.reshape(NXE, NYE, ORDER * MODES).astype(jnp.float32)


def draw_root_map(key, part):
    key_phase, key_spots, key_shift, key_coin = jax.random.split(key, 4)
    lattice_phase = jax.random.randint(key_phase, (2,), 0, 3).astype(jnp.int32)
    row_index = jnp.broadcast_to(jnp.arange(NXE, dtype=jnp.int32)[:, None], (NXE, NYE))
    col_index = jnp.broadcast_to(jnp.arange(NYE, dtype=jnp.int32)[None, :], (NXE, NYE))
    blocks_x = NXE // 3 + 2
    blocks_y = NYE // 3 + 2
    root_spots = jax.random.randint(key_spots, (blocks_x, blocks_y, 2), 0, 3).astype(jnp.int32)

    def root_at(block_x, block_y):
        block_x = jnp.clip(block_x, 0, blocks_x - 1)
        block_y = jnp.clip(block_y, 0, blocks_y - 1)
        first_x = block_x * 3 - lattice_phase[0]
        first_y = block_y * 3 - lattice_phase[1]
        spot_x = root_spots[block_x, block_y, 0]
        spot_y = root_spots[block_x, block_y, 1]
        root_x = jnp.minimum(jnp.maximum(first_x + spot_x, jnp.maximum(first_x, 0)), jnp.minimum(first_x + 2, NXE - 1))
        root_y = jnp.minimum(jnp.maximum(first_y + spot_y, jnp.maximum(first_y, 0)), jnp.minimum(first_y + 2, NYE - 1))
        usable = (first_x <= NXE - 1) & (first_y <= NYE - 1)
        return (root_x, root_y, usable)
    own_bx = (row_index + lattice_phase[0]) // 3
    own_by = (col_index + lattice_phase[1]) // 3
    own_x, own_y, own_ok = root_at(own_bx, own_by)
    moves = jax.random.randint(key_shift, (NXE, NYE, 2), -1, 2).astype(jnp.int32)
    coin_flip = jax.random.randint(key_coin, (NXE, NYE), 0, 2).astype(jnp.int32)
    cand_x, cand_y, cand_ok = root_at(own_bx + moves[..., 0], own_by + moves[..., 1])
    own_is_root = (own_x == row_index) & (own_y == col_index)
    reachable = (jnp.abs(cand_x - row_index) <= 2) & (jnp.abs(cand_y - col_index) <= 2) & cand_ok & (coin_flip == 1) & jnp.logical_not(own_is_root)
    root_x = jnp.where(reachable, cand_x, own_x)
    root_y = jnp.where(reachable, cand_y, own_y)
    return (root_x * NYE + root_y).astype(jnp.int32)


def draw_neighbours(key, part):
    steps_list = [(dx, dy) for dx in range(-2, 3) for dy in range(-2, 3) if dx != 0 or dy != 0]
    step_x = jnp.asarray(np.array([entry[0] for entry in steps_list], dtype=np.int32))
    step_y = jnp.asarray(np.array([entry[1] for entry in steps_list], dtype=np.int32))
    row_index = jnp.arange(NXE, dtype=jnp.int32)[:, None, None]
    col_index = jnp.arange(NYE, dtype=jnp.int32)[None, :, None]
    near_x = row_index + step_x[None, None, :]
    near_y = col_index + step_y[None, None, :]
    usable = (near_x >= 0) & (near_x < NXE) & (near_y >= 0) & (near_y < NYE)
    scores = jax.random.randint(key, (NXE, NYE, 24), 0, 1 << 20).astype(jnp.int32) * 32
    scores = scores + jnp.arange(24, dtype=jnp.int32)[None, None, :] + jnp.where(usable, 0, 1 << 26).astype(jnp.int32)
    picked = jnp.argsort(scores, axis=-1)[..., :COUPLINGS - 1].astype(jnp.int32)
    chosen_x = jnp.take_along_axis(jnp.broadcast_to(near_x, (NXE, NYE, 24)), picked, axis=-1)
    chosen_y = jnp.take_along_axis(jnp.broadcast_to(near_y, (NXE, NYE, 24)), picked, axis=-1)
    others = chosen_x * NYE + chosen_y
    itself = jnp.broadcast_to(row_index * NYE + col_index, (NXE, NYE, 1))
    return jnp.concatenate([itself, others], axis=-1).astype(jnp.int32)


def block_scale(key, extent, pieces, low, top_value):
    def one(position, blocks):
        heights = jax.random.uniform(jax.random.fold_in(jax.random.fold_in(key, 6), position), (blocks,), jnp.float32, low / len(pieces), top_value / len(pieces))
        return jnp.repeat(jnp.exp(heights), extent[position] // blocks).reshape((-1,) + (1,) * (len(extent) - position - 1))

    loudness = one(*pieces[0])
    for cut in pieces[1:]:
        loudness = loudness * one(*cut)
    return loudness


def gaussian(stream_key, dims, scale, bound, cuts=(), kind=jnp.bfloat16):
    level = block_scale(stream_key, dims, cuts, -0.22, 0.18) if cuts else 1.0
    result = jax.random.normal(stream_key, dims, jnp.float32) * scale * level
    return jnp.minimum(jnp.maximum(result, -bound), bound).astype(kind)


def setup_inputs(seed: int = 0) -> dict:
    seeds = jax.random.split(jax.random.key(seed), 6)
    return {
        "near_null": draw_near_null(jax.random.fold_in(seeds[5], 71), 0),
        "a_blocks": gaussian(seeds[1], (NXE, NYE, COUPLINGS, ORDER * ORDER), (ORDER * COUPLINGS) ** -0.5, 0.375, ((0, 16), (1, 8))),
        "inv_diag": jnp.clip(jnp.exp(math.log(2.0) - 1.3862944 * jax.random.uniform(seeds[2], (NXE, NYE, ORDER), jnp.float32) ** block_scale(seeds[2], (NXE, NYE, ORDER), ((0, 16), (1, 8)), -0.2, 0.2)), 0.5, 2.0),
        "root_map": draw_root_map(jax.random.fold_in(seeds[5], 71), 0),
        "neighbours": draw_neighbours(jax.random.fold_in(seeds[5], 71), 0),
    }


OMEGA = 2.0 / 3.0

def reference(near_null, a_blocks, inv_diag, root_map, neighbours):
    elements = NXE * NYE
    basis_rows = near_null.reshape(elements, ORDER, MODES)
    gram_each = jnp.einsum('nik,nil->nkl', basis_rows, basis_rows, precision=lax.Precision.HIGHEST) / ORDER
    root_list = root_map.reshape(elements).astype(jnp.int32)
    summed = jax.ops.segment_sum(gram_each.reshape(elements, MODES * MODES), root_list, num_segments=elements)
    own_index = jnp.arange(elements, dtype=jnp.int32)
    is_root = root_list == own_index
    identity = jnp.eye(MODES, dtype=jnp.float32)
    padding = jnp.where(is_root, 0.0, 1.0).astype(jnp.float32)
    matrices = summed.reshape(elements, MODES, MODES) + padding[:, None, None] * identity
    factor = jnp.linalg.cholesky(matrices)
    root_factor = jnp.take(factor, root_list, axis=0)
    solved = jax.scipy.linalg.solve_triangular(root_factor, jnp.swapaxes(basis_rows, 1, 2), lower=True)
    tentative = jnp.swapaxes(solved, 1, 2)
    tent_low = tentative.astype(jnp.bfloat16)
    table = tent_low.reshape(elements, ORDER, MODES)

    def one_row(inputs):
        row_blocks, row_links = inputs
        gathered = jnp.take(table, row_links.reshape(-1).astype(jnp.int32), axis=0)
        gathered = gathered.reshape(NYE, COUPLINGS, ORDER, MODES).astype(jnp.float32)
        row_float = row_blocks.reshape(NYE, COUPLINGS, ORDER, ORDER).astype(jnp.float32)
        return jnp.einsum('ykij,ykjc->yic', row_float, gathered, precision=lax.Precision.HIGHEST)
    applied = lax.map(one_row, (a_blocks, neighbours)).reshape(elements, ORDER, MODES)
    prolong = tentative - OMEGA * inv_diag.reshape(elements, ORDER)[:, :, None] * applied
    return prolong.reshape(NXE, NYE, ORDER * MODES)
```

```python
import functools

import jax
import jax.numpy as jnp
from jax import lax
from jax.experimental import pallas as pl
from jax.experimental.pallas import tpu as pltpu
from jax.sharding import PartitionSpec as P

F32 = jnp.float32
BF = jnp.bfloat16
OMEGA = 2.0 / 3.0

def pick_blocks(pieces, block):
    out = pieces[3]
    for b in (2, 1, 0):
        out = jnp.where(block == b, pieces[b], out)
    return out

def turn(v, s):
    s = s % 4
    return v if s == 0 else pltpu.roll(v, 32*s, 1)

def gram_kernel(xb, b_ref, g_ref, ybuf, zbuf, gbuf):
    block16 = lax.broadcasted_iota(jnp.int32, (16,128), 1)//32
    block32 = lax.broadcasted_iota(jnp.int32, (32,128), 1)//32
    block8 = lax.broadcasted_iota(jnp.int32, (8,128), 1)//32
    def one_x(xi, carry):
        for half in range(2):
            p = [b_ref[xi, pl.ds(4*half+b, 16, stride=8), :] for b in range(4)]
            for q in range(4):
                ybuf[half, pl.ds(q, 16, stride=4), :] = pick_blocks([turn(p[b], b-q) for b in range(4)], block16)
        for half in range(2):
            yh = ybuf[half].astype(BF)
            o = lax.dot_general(yh, yh, (((0,),(0,)),((),())), preferred_element_type=F32)
            zbuf[half] = pick_blocks([o[32*b:32*b+32] for b in range(4)], block32) * (1.0/64)
        for half in range(2):
            r = [zbuf[half, pl.ds(kq, 8, stride=4), :] for kq in range(4)]
            for b in range(4):
                gbuf[:, 4*half+b, :] = pick_blocks([turn(r[kq], kq-b) for kq in range(4)], block8)
        g_ref[:, xi] = gbuf[...].astype(BF)
        return carry
    lax.fori_loop(0, xb, one_x, 0)

def gram_call(nn, xb=12):
    nx = nn.shape[0]
    return pl.pallas_call(functools.partial(gram_kernel, xb), grid=(nx//xb,),
        in_specs=[pl.BlockSpec((xb,128,128), lambda i:(i,0,0))],
        out_specs=pl.BlockSpec((8,xb,8,128), lambda i:(0,i,0,0)),
        out_shape=jax.ShapeDtypeStruct((8,nx,8,128),BF),
        scratch_shapes=[pltpu.VMEM((2,64,128),F32), pltpu.VMEM((2,32,128),F32), pltpu.VMEM((8,8,128),F32)], name="gram")(nn)


def halo_kernel(nx, ny, width, xdim, ydim, with_tile, *refs):
    if with_tile:
        src, tile, dst, tiles, send, recv, own = refs
    else:
        src, dst, send, recv, own = refs
    gx, gy = lax.axis_index("gx"), lax.axis_index("gy")
    cx, cy = lax.axis_size("gx"), lax.axis_size("gy")
    sides = [(dx, dy) for dx in (-1, 0, 1) for dy in (-1, 0, 1) if dx or dy]

    def there(dx, dy):
        ok = jnp.bool_(True)
        if dx: ok &= (gx + dx >= 0) & (gx + dx < cx)
        if dy: ok &= (gy + dy >= 0) & (gy + dy < cy)
        return ok

    def taken(d, n):
        return pl.ds(0, n) if d == 0 else (pl.ds(n - width, width) if d > 0 else pl.ds(0, width))

    def landed(d, n):
        return pl.ds(width, n) if d == 0 else (pl.ds(0, width) if d > 0 else pl.ds(n + width, width))

    def view(ref, sx, sy):
        at = [slice(None)] * len(ref.shape)
        at[xdim], at[ydim] = sx, sy
        return ref.at[tuple(at)]

    def copies(s, dx, dy):
        to = (gx + dx, gy + dy)
        out = [pltpu.make_async_remote_copy(
            src_ref=view(src, taken(dx, nx), taken(dy, ny)), dst_ref=view(dst, landed(dx, nx), landed(dy, ny)),
            send_sem=send.at[0, s], recv_sem=recv.at[0, s], device_id=to, device_id_type=pl.DeviceIdType.MESH)]
        if with_tile:
            out.append(pltpu.make_async_remote_copy(
                src_ref=tile, dst_ref=tiles.at[1 - dx, 1 - dy],
                send_sem=send.at[1, s], recv_sem=recv.at[1, s], device_id=to, device_id_type=pl.DeviceIdType.MESH))
        return out

    barrier = pltpu.get_barrier_semaphore()
    for dx, dy in sides:
        @pl.when(there(dx, dy))
        def _():
            pl.semaphore_signal(barrier, inc=1, device_id=(gx + dx, gy + dy), device_id_type=pl.DeviceIdType.MESH)
    mine = [pltpu.make_async_copy(src, view(dst, pl.ds(width, nx), pl.ds(width, ny)), own.at[0])]
    if with_tile:
        mine.append(pltpu.make_async_copy(tile, tiles.at[1, 1], own.at[1]))
    for c in mine: c.start()
    wide = 1 + (gx > 0).astype(jnp.int32) + (gx < cx - 1).astype(jnp.int32)
    tall = 1 + (gy > 0).astype(jnp.int32) + (gy < cy - 1).astype(jnp.int32)
    pl.semaphore_wait(barrier, wide * tall - 1)
    for s, (dx, dy) in enumerate(sides):
        @pl.when(there(dx, dy))
        def _():
            for c in copies(s, dx, dy): c.start()
    for s, (dx, dy) in enumerate(sides):
        @pl.when(there(-dx, -dy))
        def _():
            for c in copies(s, dx, dy): c.wait_recv()
    for s, (dx, dy) in enumerate(sides):
        @pl.when(there(dx, dy))
        def _():
            for c in copies(s, dx, dy): c.wait_send()
    for c in mine: c.wait()


def halo_call(src, dst_shape, width, xdim, ydim, tile=None, collective_id=0, name="halo"):
    anyspec = pl.BlockSpec(memory_space=pl.ANY)
    outs = [jax.ShapeDtypeStruct(dst_shape, src.dtype)]
    args = [src]
    if tile is not None:
        outs.append(jax.ShapeDtypeStruct((3, 3) + tile.shape, tile.dtype))
        args.append(tile)
    n = len(args)
    return pl.pallas_call(functools.partial(halo_kernel, src.shape[xdim], src.shape[ydim], width, xdim, ydim, tile is not None),
        in_specs=[anyspec]*n, out_specs=[anyspec]*n, out_shape=outs,
        scratch_shapes=[pltpu.SemaphoreType.DMA((2,8)), pltpu.SemaphoreType.DMA((2,8)), pltpu.SemaphoreType.DMA((2,))],
        compiler_params=pltpu.CompilerParams(collective_id=collective_id, has_side_effects=True), name=name)(*args)


def factor_kernel(nx, cells_ref, slot_ref, edge_ref, rid_ref, b_ref, g_ref, t_ref, tb_ref, comp, idcol, tab, v_ref, g_buf, t16, sem):
    ncell = cells_ref.shape[0]
    px = nx + 8
    els = px * 16
    copy_g = pltpu.make_async_copy(g_ref, g_buf, sem)
    copy_g.start()
    def compact(i, n):
        cid = cells_ref[i]
        idcol[pl.ds(n, 1), :] = jnp.full((1, 128), cid, jnp.int32)
        comp[i] = n
        return n + (cid >= 0).astype(jnp.int32)
    n = lax.fori_loop(0, ncell, compact, 0, unroll=8)
    copy_g.wait()
    @pl.when(edge_ref[0] == 1)
    def _(): g_buf[:, 0:4] = jnp.zeros((8, 4, 16, 128), BF)
    @pl.when(edge_ref[1] == 1)
    def _(): g_buf[:, px-4:px] = jnp.zeros((8, 4, 16, 128), BF)
    sub16 = lax.broadcasted_iota(jnp.int32, (16, 128), 0)
    def clear(keep):
        def one(x, c):
            for k in range(8):
                g_buf[k, x] = jnp.where(keep, g_buf[k, x], jnp.zeros((16,128), BF))
            return c
        lax.fori_loop(0, px, one, 0)
    @pl.when(edge_ref[2] == 1)
    def _(): clear(sub16 >= 4)
    @pl.when(edge_ref[3] == 1)
    def _(): clear(sub16 < 12)

    sub = lax.broadcasted_iota(jnp.int32, (32, 128), 0)
    def batch(bi, c):
        base = bi*128
        ids = idcol[pl.ds(base, 128), :]
        hot = [jnp.where(ids == rid_ref[:, 128*t:128*t+128], 1.0, 0.0).astype(BF) for t in range(els//128)]
        hot = jnp.concatenate(hot, axis=1)
        for k4 in range(8):
            s = jnp.dot(hot, g_buf[k4].reshape(els, 128), preferred_element_type=F32)
            v_ref[128*k4:128*k4+128, :] = s.T
        for jb in range(4):
            def pivot(j8, c2):
                j = jb*8 + j8
                row = v_ref[pl.ds(pl.multiple_of(j*32, 32), 32), :]
                d = lax.rsqrt(v_ref[pl.ds(j*33, 1), :])
                at_j = sub == j
                u = jnp.where(at_j, d, row*d)
                v_ref[pl.ds(pl.multiple_of(j*32, 32), 32), :] = u
                keep = jnp.where(at_j, 0.0, 1.0)
                for i in range(jb*8, 32):
                    f = u[i:i+1, :]
                    old = v_ref[32*i:32*i+32, :]
                    if i < jb*8+8:
                        later = i > j
                        f = jnp.where(later, f, 0.0)
                        new = jnp.where(at_j & later, 0.0, old) - f*u
                        new = jnp.where(later, new, old)
                    else:
                        new = jnp.where(at_j, 0.0, old) - f*u
                    v_ref[32*i:32*i+32, :] = new
                return c2
            lax.fori_loop(0, 8, pivot, 0)
        for k in range(32):
            m = v_ref[pl.ds(k, 32, stride=32), :]
            m = jnp.where(sub >= k, m, 0.0)
            tab[k, pl.ds(base, 128), :] = jnp.concatenate([m]*4, axis=0).T
        return c
    lax.fori_loop(0, (n + 127)//128, batch, 0)

    block = lax.broadcasted_iota(jnp.int32, (32, 128), 1)//32
    def one_x(x, c):
        for y in range(8):
            r = comp[slot_ref[x*8+y]]
            w = tab[:, pl.ds(r, 1), :].reshape(32, 128)
            wh = w.astype(BF).astype(F32)
            wl = w - wh
            hi = jnp.concatenate([jnp.where(block == q, wh, 0.0) for q in range(4)], axis=0).astype(BF)
            lo = jnp.concatenate([jnp.where(block == q, wl, 0.0) for q in range(4)], axis=0).astype(BF)
            p = b_ref[x, pl.ds(y, 16, stride=8), :]
            ph = p.astype(BF)
            plo = (p - ph.astype(F32)).astype(BF)
            t = jnp.dot(ph, hi, preferred_element_type=F32) + jnp.dot(plo, hi, preferred_element_type=F32) + jnp.dot(ph, lo, preferred_element_type=F32)
            t_ref[x, pl.ds(y, 16, stride=8), :] = t
            tb_ref[x, y] = t.astype(BF)
        return c
    lax.fori_loop(0, nx, one_x, 0)

def factor_call(cells, slots, edge, rid, nn, gpad):
    nx = nn.shape[0]
    full = lambda s: pl.BlockSpec(s, lambda i,*_: (0,)*len(s), pipeline_mode=pl.Buffered(1))
    nc = (nx+4)*12
    ncp = (nc + 127)//128*128 + 128
    return pl.pallas_call(functools.partial(factor_kernel, nx),
        grid_spec=pltpu.PrefetchScalarGridSpec(num_scalar_prefetch=3, grid=(1,),
          in_specs=[full(rid.shape), full(nn.shape), pl.BlockSpec(memory_space=pl.ANY)],
          out_specs=[full(nn.shape), full((nx,8,16,128))],
          scratch_shapes=[pltpu.SMEM((nc,), jnp.int32), pltpu.VMEM((ncp,128), jnp.int32), pltpu.VMEM((32,ncp,128),F32), pltpu.VMEM((1024,128),F32), pltpu.VMEM(gpad.shape,BF), pltpu.VMEM((16,128),F32), pltpu.SemaphoreType.DMA]),
        out_shape=[jax.ShapeDtypeStruct(nn.shape,F32), jax.ShapeDtypeStruct((nx,8,16,128),BF)],
        compiler_params=pltpu.CompilerParams(vmem_limit_bytes=56<<20), name="factor")(cells, slots, edge, rid, nn, gpad)


def apply_kernel(nx, px, py, xb, idx_ref, t_ref, d_ref, sel_ref, tp_ref, a_ref, out_ref, abuf, table, wide, tall, scale_ref, sems):
    step = pl.program_id(0)
    steps = nx // xb
    def copies(s, slot):
        return [pltpu.make_async_copy(a_ref.at[pl.ds(s*xb, xb), :, :, pl.ds(2*kp, 2), :], abuf.at[slot, :, :, kp], sems.at[slot, kp]) for kp in range(2)]
    lane = lax.broadcasted_iota(jnp.int32, (16, 128), 1)
    @pl.when(step == 0)
    def _():
        for c in copies(0, 0): c.start()
        def expand(x, carry):
            rows = tp_ref[x].reshape(py*16, 128)
            o = jnp.dot(rows, sel_ref[...], preferred_element_type=F32)
            for y in range(py):
                for q in range(4):
                    tall[y, pl.ds(q, 16, stride=4), :] = o[y*16:(y+1)*16, q*128:(q+1)*128]
            for y in range(py):
                table[x*py+y] = tall[y].astype(BF)
            return carry
        lax.fori_loop(0, px, expand, 0)
    slot = lax.rem(step, 2)
    @pl.when(step + 1 < steps)
    def _():
        for c in copies(step+1, 1-slot): c.start()
    for c in copies(step, slot): c.wait()
    row8 = lax.broadcasted_iota(jnp.int32, (128, 64), 0) // 8
    col4 = lax.broadcasted_iota(jnp.int32, (128, 64), 1) // 4
    pick = (lax.broadcasted_iota(jnp.int32, (64, 128), 0) % 4 == lax.broadcasted_iota(jnp.int32, (64, 128), 1) // 32)
    pick = jnp.where(pick, 1.0, 0.0).astype(BF)
    lanew = lax.broadcasted_iota(jnp.int32, (64, 128), 1)
    def one_x(xi, carry):
        d = d_ref[xi] * OMEGA
        dt = jnp.where(row8 == col4, jnp.concatenate([d]*16, axis=0), 0.0)
        hi = dt.astype(BF); lo = (dt - hi.astype(F32)).astype(BF)
        scale_ref[...] = jnp.dot(hi, pick, preferred_element_type=F32) + jnp.dot(lo, pick, preferred_element_type=F32)
        for y in range(8):
            e4 = ((step*xb + xi)*8 + y)*4
            parts = []
            for kp in range(2):
                t0 = table[idx_ref[e4+2*kp]]
                t1 = table[idx_ref[e4+2*kp+1]]
                r = jnp.where(lanew < 64, t0, t1)
                parts.append(jnp.where((lanew//32) % 2 == 0, r, jnp.zeros_like(r)))
                parts.append(jnp.where((lanew//32) % 2 == 1, r, jnp.zeros_like(r)))
            rhs = jnp.concatenate(parts, axis=0)
            lhs = jnp.concatenate([abuf[slot, xi, y, 0].reshape(64,128), abuf[slot, xi, y, 1].reshape(64,128)], axis=1)
            wide[y] = jnp.dot(lhs, rhs, preferred_element_type=F32)
        for y in range(8):
            r = [wide[y, pl.ds(q, 16, stride=4), :] for q in range(4)]
            u = jnp.where(lane < 64, r[0], r[3]) + pltpu.roll(jnp.where(lane < 64, r[2], r[1]), 64, 1)
            rows = pl.ds(y, 16, stride=8)
            out_ref[xi, rows, :] = t_ref[xi, rows, :] - scale_ref[rows, :] * u
        return carry
    lax.fori_loop(0, xb, one_x, 0)

def spread_matrix():
    r = jnp.arange(128)[:, None]; c = jnp.arange(512)[None, :]
    return ((r//32 == c//128) & (r%32 == c%32)).astype(BF)

def apply_call(idx, t4, d, tp, a5, xb=4):
    nx = t4.shape[0]; px, py = tp.shape[:2]
    blk = pl.BlockSpec((xb,128,128), lambda i,*_:(i,0,0))
    return pl.pallas_call(functools.partial(apply_kernel, nx, px, py, xb),
        grid_spec=pltpu.PrefetchScalarGridSpec(num_scalar_prefetch=1, grid=(nx//xb,),
          in_specs=[blk, pl.BlockSpec((xb,8,64), lambda i,*_:(i,0,0)), pl.BlockSpec((128,512), lambda i,*_:(0,0)),
                    pl.BlockSpec((px,py,16,128), lambda i,*_:(0,0,0,0), pipeline_mode=pl.Buffered(1)), pl.BlockSpec(memory_space=pl.ANY)],
          out_specs=blk,
          scratch_shapes=[pltpu.VMEM((2,xb,8,2,32,2,128),BF), pltpu.VMEM((px*py,64,128),BF), pltpu.VMEM((8,64,128),F32), pltpu.VMEM((py,64,128),F32), pltpu.VMEM((128,128),F32), pltpu.SemaphoreType.DMA((2,2))]),
        out_shape=jax.ShapeDtypeStruct((nx,128,128),F32),
        compiler_params=pltpu.CompilerParams(vmem_limit_bytes=56<<20), name="apply")(idx, t4, d, spread_matrix(), tp, a5)


def body(near_null, a_blocks, inv_diag, root_map, neighbours):
    nx, ny = root_map.shape
    grid_x, grid_y = nx * lax.axis_size("gx"), ny * lax.axis_size("gy")
    gx, gy = lax.axis_index("gx"), lax.axis_index("gy")
    sx, sy = gx * nx, gy * ny
    nn = near_null.reshape(nx, ny, 16, 128).transpose(0, 2, 1, 3).reshape(nx, 128, 128)
    a5 = a_blocks.reshape(nx, ny, 4, 32, 128).transpose(0, 1, 3, 2, 4)
    tile = jnp.pad(root_map.T, ((0, 0), (0, 128 - nx)))
    grams = gram_call(nn)
    gpad, tiles = halo_call(grams, (8, nx + 8, ny + 8, 128), 4, 1, 2, tile=tile, collective_id=0, name="halo_gram")
    around = tiles[:, :, :, :nx].transpose(0, 3, 1, 2).reshape(3 * nx, 3 * ny)[nx - 4:2 * nx + 4, ny - 4:2 * ny + 4]
    ax = sx - 4 + jnp.arange(nx + 8, dtype=jnp.int32)[:, None]
    ay = sy - 4 + jnp.arange(ny + 8, dtype=jnp.int32)[None, :]
    around = jnp.where((ax >= 0) & (ax < grid_x) & (ay >= 0) & (ay < grid_y), around, -1)
    cells = jnp.where(around == ax * grid_y + ay, around, -1)[2:-2, 2:-2].reshape(-1)
    slots = ((root_map // grid_y - sx + 2) * (ny + 4) + root_map % grid_y - sy + 2).reshape(-1)
    edge = jnp.stack([gx == 0, gx == lax.axis_size("gx") - 1, gy == 0, gy == lax.axis_size("gy") - 1]).astype(jnp.int32)
    tent, low = factor_call(cells, slots, edge, around.reshape(1, -1), nn, gpad)
    (low_pad,) = halo_call(low, (nx + 4, ny + 4, 16, 128), 2, 0, 1, collective_id=1, name="halo_tent")
    idx = ((neighbours // grid_y - sx + 2) * (ny + 4) + neighbours % grid_y - sy + 2).reshape(-1)
    out = apply_call(idx, tent, inv_diag, low_pad, a5)
    return out.reshape(nx, 16, ny, 128).transpose(0, 2, 1, 3).reshape(nx, ny, 2048)


def solution(mesh):
    in_specs = (P("gx", "gy", None), P("gx", "gy", None, None), P("gx", "gy", None), P("gx", "gy"), P("gx", "gy", None))
    return jax.shard_map(body, mesh=mesh, in_specs=in_specs, out_specs=P("gx", "gy", None), check_vma=False)
```

```python
import functools

import jax
import jax.numpy as jnp
from jax import lax
from jax.experimental import pallas as pl
from jax.experimental.pallas import tpu as pltpu
from jax.sharding import PartitionSpec as P

F32 = jnp.float32
BF = jnp.bfloat16
OMEGA = 2.0 / 3.0

SIDES = [(dx, dy) for dx in (-1, 0, 1) for dy in (-1, 0, 1) if dx or dy]


def there(dx, dy):
    gx, gy = lax.axis_index("gx"), lax.axis_index("gy")
    ok = jnp.bool_(True)
    if dx:
        ok &= (gx + dx >= 0) & (gx + dx < lax.axis_size("gx"))
    if dy:
        ok &= (gy + dy >= 0) & (gy + dy < lax.axis_size("gy"))
    return ok


def peer(dx, dy):
    return (lax.axis_index("gx") + dx, lax.axis_index("gy") + dy)


def remote(src, dst, send, recv, to):
    return pltpu.make_async_remote_copy(src_ref=src, dst_ref=dst, send_sem=send, recv_sem=recv, device_id=to, device_id_type=pl.DeviceIdType.MESH)


def greet():
    for dx, dy in SIDES:
        @pl.when(there(dx, dy))
        def _():
            pl.semaphore_signal(pltpu.get_barrier_semaphore(), inc=1, device_id=peer(dx, dy), device_id_type=pl.DeviceIdType.MESH)


def meet():
    gx, gy = lax.axis_index("gx"), lax.axis_index("gy")
    wide = 1 + (gx > 0).astype(jnp.int32) + (gx < lax.axis_size("gx") - 1).astype(jnp.int32)
    tall = 1 + (gy > 0).astype(jnp.int32) + (gy < lax.axis_size("gy") - 1).astype(jnp.int32)
    pl.semaphore_wait(pltpu.get_barrier_semaphore(), wide * tall - 1)


def exchange_start(copies):
    for s, (dx, dy) in enumerate(SIDES):
        @pl.when(there(dx, dy))
        def _():
            for c in copies(s, dx, dy, peer(dx, dy)):
                c.start()


def exchange_wait(copies):
    for s, (dx, dy) in enumerate(SIDES):
        @pl.when(there(-dx, -dy))
        def _():
            for c in copies(s, dx, dy, peer(dx, dy)):
                c.wait_recv()
    for s, (dx, dy) in enumerate(SIDES):
        @pl.when(there(dx, dy))
        def _():
            for c in copies(s, dx, dy, peer(dx, dy)):
                c.wait_send()


def exchange(copies):
    exchange_start(copies)
    exchange_wait(copies)


def halo_kernel(nx, ny, width, src, dst, send, recv):
    def taken(d, n):
        return {0: pl.ds(0, n), 1: pl.ds(n - width, width), -1: pl.ds(0, width)}[d]

    def landed(d, n):
        return {0: pl.ds(width, n), 1: pl.ds(0, width), -1: pl.ds(n + width, width)}[d]

    def copies(s, dx, dy, to):
        return [remote(src.at[taken(dx, nx), taken(dy, ny)], dst.at[landed(dx, nx), landed(dy, ny)], send.at[s], recv.at[s], to)]

    greet()
    meet()
    exchange(copies)


def halo_call(src, dst_shape, width):
    anyspec = pl.BlockSpec(memory_space=pl.ANY)
    return pl.pallas_call(functools.partial(halo_kernel, src.shape[0], src.shape[1], width),
        in_specs=[anyspec], out_specs=anyspec, out_shape=jax.ShapeDtypeStruct(dst_shape, src.dtype),
        scratch_shapes=[pltpu.SemaphoreType.DMA((8,)), pltpu.SemaphoreType.DMA((8,))],
        compiler_params=pltpu.CompilerParams(collective_id=1, has_side_effects=True), name="halo")(src)


def pick_blocks(pieces, block):
    out = pieces[3]
    for b in (2, 1, 0):
        out = jnp.where(block == b, pieces[b], out)
    return out


def turn(v, s):
    s = s % 4
    return v if s == 0 else pltpu.roll(v, 32*s, 1)


def gram_rows(x, p_buf, z_buf, g_buf, low_buf, slot):
    block16 = lax.broadcasted_iota(jnp.int32, (16,128), 1)//32
    block8 = lax.broadcasted_iota(jnp.int32, (8,128), 1)//32
    for half in range(2):
        p = [p_buf[x, 4*half+b] for b in range(4)]
        yh = jnp.concatenate([pick_blocks([turn(p[b], b-q) for b in range(4)], block16) for q in range(4)], axis=0)
        hi = yh.astype(BF)
        lo = (yh - hi.astype(F32)).astype(BF)
        o = lax.dot_general(jnp.concatenate([hi, lo, hi], axis=0), jnp.concatenate([hi, hi, lo], axis=0), (((0,),(0,)),((),())), preferred_element_type=F32)
        r = [pick_blocks([o[32*b+8*kb:32*b+8*kb+8] for b in range(4)], block8) * (1.0/64) for kb in range(4)]
        for b in range(4):
            z_buf[slot, :, b, :] = pick_blocks([turn(r[kb], kb-b) for kb in range(4)], block8)
        z = z_buf[slot]
        zh = z.astype(BF)
        g_buf[half, :, x] = zh
        low_buf[half, :, x] = (z - zh.astype(F32)).astype(BF)


def gram_kernel(nx, chunks, with_halo, *refs):
    if with_halo:
        b_ref, tile, gpad, glow, tiles, p_buf, z_buf, g_buf, low_buf, load, store, send, recv = refs
    else:
        b_ref, gpad, glow, p_buf, z_buf, g_buf, low_buf, load, store = refs
    part = nx // chunks
    loads = [[pltpu.make_async_copy(b_ref.at[pl.ds(c*part, part), :, y], p_buf.at[pl.ds(c*part, part), y], load.at[c, y]) for y in range(8)] for c in range(chunks)]
    for group in loads:
        for c in group: c.start()
    if with_halo:
        greet()
    for c in range(chunks):
        for one in loads[c]: one.wait()
        def rows(i, carry):
            for u in range(2):
                gram_rows(c*part + 2*i + u, p_buf, z_buf, g_buf, low_buf, u)
            return carry
        lax.fori_loop(0, part//2, rows, 0)
    mine = pltpu.make_async_copy(g_buf, gpad.at[pl.ds(1, 2), :, pl.ds(4, nx)], store.at[0])
    low = pltpu.make_async_copy(low_buf, glow, store.at[2])
    mine.start()
    low.start()
    if with_halo:
        meet()
        def strip(ref, sx, sy):
            return ref.at[sy, :, sx]
        def copies(s, dx, dy, to):
            sx = {0: pl.ds(0, nx), 1: pl.ds(nx-4, 4), -1: pl.ds(0, 4)}[dx]
            sy = {0: pl.ds(0, 2), 1: pl.ds(1, 1), -1: pl.ds(0, 1)}[dy]
            tx = {0: pl.ds(4, nx), 1: pl.ds(0, 4), -1: pl.ds(nx+4, 4)}[dx]
            ty = {0: pl.ds(1, 2), 1: pl.ds(0, 1), -1: pl.ds(3, 1)}[dy]
            return [remote(strip(g_buf, sx, sy), strip(gpad, tx, ty), send.at[0, s], recv.at[0, s], to),
                    remote(tile, tiles.at[1-dx, 1-dy], send.at[1, s], recv.at[1, s], to)]
        own_tile = pltpu.make_async_copy(tile, tiles.at[1, 1], store.at[1])
        own_tile.start()
        exchange(copies)
        own_tile.wait()
    mine.wait()
    low.wait()


def gram_call(nn, tile=None, chunks=4):
    nx = nn.shape[0]
    anyspec = pl.BlockSpec(memory_space=pl.ANY)
    gshape = jax.ShapeDtypeStruct((4, 8, nx+8, 4, 128), BF)
    scratch = [pltpu.VMEM((nx,8,16,128),F32), pltpu.VMEM((2,8,4,128),F32), pltpu.VMEM((2,8,nx,4,128),BF), pltpu.VMEM((2,8,nx,4,128),BF),
               pltpu.SemaphoreType.DMA((chunks,8)), pltpu.SemaphoreType.DMA((3,))]
    lshape = jax.ShapeDtypeStruct((2, 8, nx, 4, 128), BF)
    kern = functools.partial(gram_kernel, nx, chunks, tile is not None)
    if tile is None:
        return pl.pallas_call(kern, in_specs=[anyspec], out_specs=[anyspec]*2, out_shape=[gshape, lshape], scratch_shapes=scratch,
            compiler_params=pltpu.CompilerParams(vmem_limit_bytes=56<<20), name="gram")(nn)
    return pl.pallas_call(kern, in_specs=[anyspec]*2, out_specs=[anyspec]*3,
        out_shape=[gshape, lshape, jax.ShapeDtypeStruct((3,3)+tile.shape, tile.dtype)],
        scratch_shapes=scratch + [pltpu.SemaphoreType.DMA((2,8)), pltpu.SemaphoreType.DMA((2,8))],
        compiler_params=pltpu.CompilerParams(vmem_limit_bytes=56<<20, collective_id=0, has_side_effects=True), name="gram")(nn, tile)


def factor_kernel(nx, cells_ref, slot_ref, edge_ref, rid_ref, b_ref, g_ref, gl_ref, t_ref, tb_ref, comp, idcol, tab, bd, v_ref, g_buf, gl_buf, p_buf, t_buf, tb_buf, sem, load, store):
    ncell = cells_ref.shape[0]
    px = nx + 8
    els = rid_ref.shape[1]
    chunks = 4
    part = nx // chunks
    copies_g = [pltpu.make_async_copy(g_ref, g_buf, sem.at[0]), pltpu.make_async_copy(gl_ref, gl_buf, sem.at[1])]
    for c in copies_g: c.start()
    loads = [pltpu.make_async_copy(b_ref.at[:, :, y], p_buf.at[:, y], load.at[y]) for y in range(8)]
    for c in loads: c.start()
    def compact(i, n):
        cid = cells_ref[i]
        idcol[pl.ds(n, 1), :] = jnp.full((1, 128), cid, jnp.int32)
        comp[i] = n
        return n + (cid >= 0).astype(jnp.int32)
    n = lax.fori_loop(0, ncell, compact, 0, unroll=8)
    for c in copies_g: c.wait()
    @pl.when(edge_ref[0] == 1)
    def _(): g_buf[:, :, 0:4] = jnp.zeros((4, 8, 4, 4, 128), BF)
    @pl.when(edge_ref[1] == 1)
    def _(): g_buf[:, :, px-4:px] = jnp.zeros((4, 8, 4, 4, 128), BF)
    @pl.when(edge_ref[2] == 1)
    def _(): g_buf[0] = jnp.zeros((8, px, 4, 128), BF)
    @pl.when(edge_ref[3] == 1)
    def _(): g_buf[3] = jnp.zeros((8, px, 4, 128), BF)

    sub = lax.broadcasted_iota(jnp.int32, (32, 128), 0)
    block = lax.broadcasted_iota(jnp.int32, (32, 128), 1)//32
    def batch(bi, c):
        base = bi*128
        ids = idcol[pl.ds(base, 128), :]
        hot = [jnp.where(ids == rid_ref[:, 128*t:128*t+128], 1.0, 0.0).astype(BF) for t in range(els//128)]
        hot = jnp.concatenate(hot, axis=1)
        for k8 in range(8):
            g = jnp.concatenate([g_buf[yb, k8].reshape(px*4, 128) for yb in range(4)] + [gl_buf[yb, k8].reshape(nx*4, 128) for yb in range(2)], axis=0)
            s = jnp.dot(hot, g, preferred_element_type=F32).T
            for kb in range(4):
                v_ref[32*(8*kb+k8):32*(8*kb+k8)+32, :] = s[32*kb:32*kb+32]
        for jb in range(4):
            def pivot(j8, c2):
                j = jb*8 + j8
                row = v_ref[pl.ds(pl.multiple_of(j*32, 32), 32), :]
                d = lax.rsqrt(v_ref[pl.ds(j*33, 1), :])
                at_j = sub == j
                u = jnp.where(at_j, d, row*d)
                v_ref[pl.ds(pl.multiple_of(j*32, 32), 32), :] = u
                for i in range(jb*8, 32):
                    f = u[i:i+1, :]
                    old = v_ref[32*i:32*i+32, :]
                    if i < jb*8+8:
                        later = i > j
                        f = jnp.where(later, f, 0.0)
                        new = jnp.where(at_j & later, 0.0, old) - f*u
                        new = jnp.where(later, new, old)
                    else:
                        new = jnp.where(at_j, 0.0, old) - f*u
                    v_ref[32*i:32*i+32, :] = new
                return c2
            lax.fori_loop(0, 8, pivot, 0)
        for k in range(32):
            m = v_ref[pl.ds(k, 32, stride=32), :]
            m = jnp.where(sub >= k, m, 0.0)
            tab[k] = jnp.concatenate([m]*4, axis=0).T
        def spread(r, c2):
            w = tab[:, pl.ds(r, 1), :].reshape(32, 128)
            hi = w.astype(BF)
            lo = (w - hi.astype(F32)).astype(BF)
            for q in range(4):
                bd[base + r, 32*q:32*q+32, :] = jnp.where(block == q, hi, jnp.zeros_like(hi))
                bd[base + r, 128+32*q:160+32*q, :] = jnp.where(block == q, lo, jnp.zeros_like(lo))
            return c2
        lax.fori_loop(0, jnp.minimum(n - base, 128), spread, 0)
        return c
    lax.fori_loop(0, (n + 127)//128, batch, 0)

    for c in loads: c.wait()
    stores = []
    for ch in range(chunks):
        def one_x(i, c):
            x = ch*part + i
            for y in range(8):
                r = comp[slot_ref[x*8+y]]
                p = p_buf[x, y]
                ph = p.astype(BF)
                plo = (p - ph.astype(F32)).astype(BF)
                lhs = jnp.concatenate([jnp.concatenate([ph, ph], axis=1), jnp.concatenate([plo, jnp.zeros_like(plo)], axis=1)], axis=0)
                o = jnp.dot(lhs, bd[r], preferred_element_type=F32)
                t = o[:16] + o[16:]
                t_buf[x, y] = t
                tb_buf[x, y] = t.astype(BF)
            return c
        lax.fori_loop(0, part, one_x, 0)
        xs = pl.ds(ch*part, part)
        for c in (pltpu.make_async_copy(t_buf.at[xs], t_ref.at[xs], store.at[0, ch]), pltpu.make_async_copy(tb_buf.at[xs], tb_ref.at[xs], store.at[1, ch])):
            c.start()
            stores.append(c)
    for c in stores: c.wait()


def factor_call(cells, slots, edge, rid, nn, gpad, glow):
    nx = nn.shape[0]
    anyspec = pl.BlockSpec(memory_space=pl.ANY)
    nc = (nx+4)*12
    ncp = (nc + 127)//128*128
    return pl.pallas_call(functools.partial(factor_kernel, nx),
        grid_spec=pltpu.PrefetchScalarGridSpec(num_scalar_prefetch=3, grid=(1,),
          in_specs=[pl.BlockSpec(rid.shape, lambda i,*_: (0,0)), anyspec, anyspec, anyspec],
          out_specs=[anyspec, anyspec],
          scratch_shapes=[pltpu.SMEM((nc,), jnp.int32), pltpu.VMEM((ncp+128,128), jnp.int32), pltpu.VMEM((32,128,128),F32), pltpu.VMEM((ncp,256,128),BF),
             pltpu.VMEM((1024,128),F32), pltpu.VMEM(gpad.shape,BF), pltpu.VMEM(glow.shape,BF), pltpu.VMEM((nx,8,16,128),F32), pltpu.VMEM((nx,8,16,128),F32), pltpu.VMEM((nx,8,16,128),BF),
             pltpu.SemaphoreType.DMA((2,)), pltpu.SemaphoreType.DMA((8,)), pltpu.SemaphoreType.DMA((2,4))]),
        out_shape=[jax.ShapeDtypeStruct((nx,8,16,128),F32), jax.ShapeDtypeStruct((nx,8,16,128),BF)],
        compiler_params=pltpu.CompilerParams(vmem_limit_bytes=62<<20), name="factor")(cells, slots, edge, rid, nn, gpad, glow)


def apply_kernel(nx, px, py, xb, idx_ref, t_ref, d_ref, sel_ref, own_ref, tp_ref, a_ref, out_ref, abuf, table, wide, tall, scale_ref, tbuf, obuf, sems, osem, tsem):
    step = pl.program_id(0)
    steps = nx // xb
    slot = lax.rem(step, 2)
    def copies(s, slot):
        return [pltpu.make_async_copy(a_ref.at[pl.ds(s*xb, xb), :, :, ch, pl.ds(2*kp, 2), :], abuf.at[slot, :, :, kp, ch], sems.at[slot, 2*kp+ch]) for kp in range(2) for ch in range(2)]
    def outs(s, slot):
        return [pltpu.make_async_copy(obuf.at[slot, :, y], out_ref.at[pl.ds(s*xb, xb), :, y], osem.at[slot, y]) for y in range(8)]
    lane = lax.broadcasted_iota(jnp.int32, (16, 128), 1)
    @pl.when(step == 0)
    def _():
        strips = [(pl.ds(0, 2), pl.ds(0, py)), (pl.ds(px-2, 2), pl.ds(0, py)), (pl.ds(2, nx), pl.ds(0, 2)), (pl.ds(2, nx), pl.ds(py-2, 2))]
        fill = [pltpu.make_async_copy(tp_ref.at[sx, sy], tbuf.at[sx, sy], tsem.at[i]) for i, (sx, sy) in enumerate(strips)]
        fill.append(pltpu.make_async_copy(own_ref, tbuf.at[pl.ds(2, nx), pl.ds(2, py-4)], tsem.at[4]))
        for c in fill: c.start()
        for c in copies(0, 0): c.start()
        for c in fill: c.wait()
        def expand(x, carry):
            rows = tbuf[x].reshape(py*16, 128)
            o = jnp.dot(rows, sel_ref[...], preferred_element_type=F32)
            for y in range(py):
                for q in range(4):
                    tall[y, pl.ds(q, 16, stride=4), :] = o[y*16:(y+1)*16, q*128:(q+1)*128]
            for y in range(py):
                table[x*py+y] = tall[y].astype(BF)
            return carry
        lax.fori_loop(0, px, expand, 0)
    @pl.when(step + 1 < steps)
    def _():
        for c in copies(step+1, 1-slot): c.start()
    @pl.when(step >= 2)
    def _():
        for c in outs(step-2, slot): c.wait()
    for c in copies(step, slot): c.wait()
    row16 = lax.broadcasted_iota(jnp.int32, (16, 128), 0)
    col4 = (lax.broadcasted_iota(jnp.int32, (16, 128), 1) % 64) // 4
    pick = (lax.broadcasted_iota(jnp.int32, (64, 128), 0) % 4 == lax.broadcasted_iota(jnp.int32, (64, 128), 1) // 32)
    pick = jnp.where(pick, 1.0, 0.0).astype(BF)
    pick = jnp.concatenate([pick, pick], axis=0)
    lanew = lax.broadcasted_iota(jnp.int32, (64, 128), 1)
    def one_x(xi, carry):
        d = d_ref[xi] * OMEGA
        hi = d.astype(BF).astype(F32)
        both = jnp.concatenate([hi, d - hi], axis=1)
        spread = jnp.concatenate([jnp.where(row16 == col4, both[y:y+1], 0.0) for y in range(8)], axis=0)
        scale_ref[...] = jnp.dot(spread.astype(BF), pick, preferred_element_type=F32)
        for y in range(8):
            e4 = ((step*xb + xi)*8 + y)*4
            parts = []
            for kp in range(2):
                t0 = table[idx_ref[e4+2*kp]]
                t1 = table[idx_ref[e4+2*kp+1]]
                r = jnp.where(lanew < 64, t0, t1)
                parts.append(jnp.where((lanew//32) % 2 == 0, r, jnp.zeros_like(r)))
                parts.append(jnp.where((lanew//32) % 2 == 1, r, jnp.zeros_like(r)))
            rhs = jnp.concatenate(parts, axis=0)
            lhs = jnp.concatenate([abuf[slot, xi, y, 0].reshape(64,128), abuf[slot, xi, y, 1].reshape(64,128)], axis=1)
            wide[y] = jnp.dot(lhs, rhs, preferred_element_type=F32)
        for y in range(8):
            r = [[wide[y, pl.ds(32*ch+p, 16, stride=2), :] for p in range(2)] for ch in range(2)]
            u = jnp.where(lane < 64, r[0][0], r[1][1]) + pltpu.roll(jnp.where(lane < 64, r[1][0], r[0][1]), 64, 1)
            obuf[slot, xi, y] = t_ref[xi, y] - scale_ref[16*y:16*y+16, :] * u
        return carry
    lax.fori_loop(0, xb, one_x, 0)
    for c in outs(step, slot): c.start()
    @pl.when(step == steps - 1)
    def _():
        for c in outs(step-1, 1-slot) + outs(step, slot): c.wait()


def spread_matrix():
    r = jnp.arange(128)[:, None]; c = jnp.arange(512)[None, :]
    return ((r//32 == c//128) & (r%32 == c%32)).astype(BF)


def apply_call(idx, t4, d, own, tp, a6, xb=4):
    nx = t4.shape[0]; px, py = tp.shape[:2]
    anyspec = pl.BlockSpec(memory_space=pl.ANY)
    return pl.pallas_call(functools.partial(apply_kernel, nx, px, py, xb),
        grid_spec=pltpu.PrefetchScalarGridSpec(num_scalar_prefetch=1, grid=(nx//xb,),
          in_specs=[pl.BlockSpec((xb,8,16,128), lambda i,*_:(i,0,0,0)), pl.BlockSpec((xb,8,64), lambda i,*_:(i,0,0)), pl.BlockSpec((128,512), lambda i,*_:(0,0)),
                    anyspec, anyspec, anyspec],
          out_specs=anyspec,
          scratch_shapes=[pltpu.VMEM((2,xb,8,2,2,16,2,128),BF), pltpu.VMEM((px*py,64,128),BF), pltpu.VMEM((8,64,128),F32), pltpu.VMEM((py,64,128),F32), pltpu.VMEM((128,128),F32),
             pltpu.VMEM((px,py,16,128),BF), pltpu.VMEM((2,xb,8,16,128),F32), pltpu.SemaphoreType.DMA((2,4)), pltpu.SemaphoreType.DMA((2,8)), pltpu.SemaphoreType.DMA((5,))]),
        out_shape=jax.ShapeDtypeStruct((nx,16,8,128),F32),
        compiler_params=pltpu.CompilerParams(vmem_limit_bytes=56<<20), name="apply")(idx, t4, d, spread_matrix(), own, tp, a6)


def body(near_null, a_blocks, inv_diag, root_map, neighbours):
    nx, ny = root_map.shape
    grid_x, grid_y = nx * lax.axis_size("gx"), ny * lax.axis_size("gy")
    gx, gy = lax.axis_index("gx"), lax.axis_index("gy")
    sx, sy = gx * nx, gy * ny
    nn = near_null.reshape(nx, ny, 16, 128).transpose(0, 2, 1, 3)
    a6 = a_blocks.reshape(nx, ny, 4, 16, 2, 128).transpose(0, 1, 3, 4, 2, 5)
    tile = jnp.pad(root_map.T, ((0, 0), (0, 128 - nx)))
    gpad, glow, tiles = gram_call(nn, tile)
    around = tiles[:, :, :, :nx].transpose(0, 3, 1, 2).reshape(3 * nx, 3 * ny)[nx - 4:2 * nx + 4, ny - 4:2 * ny + 4]
    ax = sx - 4 + jnp.arange(nx + 8, dtype=jnp.int32)[:, None]
    ay = sy - 4 + jnp.arange(ny + 8, dtype=jnp.int32)[None, :]
    around = jnp.where((ax >= 0) & (ax < grid_x) & (ay >= 0) & (ay < grid_y), around, -1)
    cells = jnp.where(around == ax * grid_y + ay, around, -1)[2:-2, 2:-2].reshape(-1)
    rid = jnp.concatenate([around.reshape(nx + 8, 4, 4).transpose(1, 0, 2).reshape(1, -1), root_map.reshape(nx, 2, 4).transpose(1, 0, 2).reshape(1, -1)], axis=1)
    slots = ((root_map // grid_y - sx + 2) * (ny + 4) + root_map % grid_y - sy + 2).reshape(-1)
    edge = jnp.stack([gx == 0, gx == lax.axis_size("gx") - 1, gy == 0, gy == lax.axis_size("gy") - 1]).astype(jnp.int32)
    tent, low = factor_call(cells, slots, edge, rid, nn, gpad, glow)
    low_pad = halo_call(low, (nx + 4, ny + 4, 16, 128), 2)
    idx = ((neighbours // grid_y - sx + 2) * (ny + 4) + neighbours % grid_y - sy + 2).reshape(-1)
    out = apply_call(idx, tent, inv_diag, low, low_pad, a6)
    return out.transpose(0, 2, 1, 3).reshape(nx, ny, 2048)


def solution(mesh):
    in_specs = (P("gx", "gy", None), P("gx", "gy", None, None), P("gx", "gy", None), P("gx", "gy"), P("gx", "gy", None))
    return jax.shard_map(body, mesh=mesh, in_specs=in_specs, out_specs=P("gx", "gy", None), check_vma=False)
```

```python
import functools

import jax
import jax.numpy as jnp
from jax import lax
from jax.experimental import pallas as pl
from jax.experimental.pallas import tpu as pltpu
from jax.sharding import PartitionSpec as P

F32 = jnp.float32
BF = jnp.bfloat16
OMEGA = 2.0 / 3.0

SIDES = [(dx, dy) for dx in (-1, 0, 1) for dy in (-1, 0, 1) if dx or dy]


def there(dx, dy):
    gx, gy = lax.axis_index("gx"), lax.axis_index("gy")
    ok = jnp.bool_(True)
    if dx:
        ok &= (gx + dx >= 0) & (gx + dx < lax.axis_size("gx"))
    if dy:
        ok &= (gy + dy >= 0) & (gy + dy < lax.axis_size("gy"))
    return ok


def peer(dx, dy):
    return (lax.axis_index("gx") + dx, lax.axis_index("gy") + dy)


def remote(src, dst, send, recv, to):
    return pltpu.make_async_remote_copy(src_ref=src, dst_ref=dst, send_sem=send, recv_sem=recv, device_id=to, device_id_type=pl.DeviceIdType.MESH)


def greet():
    for dx, dy in SIDES:
        @pl.when(there(dx, dy))
        def _():
            pl.semaphore_signal(pltpu.get_barrier_semaphore(), inc=1, device_id=peer(dx, dy), device_id_type=pl.DeviceIdType.MESH)


def meet():
    gx, gy = lax.axis_index("gx"), lax.axis_index("gy")
    wide = 1 + (gx > 0).astype(jnp.int32) + (gx < lax.axis_size("gx") - 1).astype(jnp.int32)
    tall = 1 + (gy > 0).astype(jnp.int32) + (gy < lax.axis_size("gy") - 1).astype(jnp.int32)
    pl.semaphore_wait(pltpu.get_barrier_semaphore(), wide * tall - 1)


def send_all(messages, phase):
    for at, dx, dy, copy in messages:
        if at == phase:
            @pl.when(there(dx, dy))
            def _():
                copy(peer(dx, dy)).start()


def wait_all(messages):
    for _, dx, dy, copy in messages:
        @pl.when(there(-dx, -dy))
        def _():
            copy(peer(dx, dy)).wait_recv()
    for _, dx, dy, copy in messages:
        @pl.when(there(dx, dy))
        def _():
            copy(peer(dx, dy)).wait_send()


def spread_lanes():
    r = lax.broadcasted_iota(jnp.int32, (128, 512), 0)
    c = lax.broadcasted_iota(jnp.int32, (128, 512), 1)
    return jnp.where((r // 32 == c // 128) & (r % 32 == c % 32), 1.0, 0.0).astype(BF)


def expanded(rows, fan_ref, tall):
    o = jnp.dot(rows, fan_ref[...], preferred_element_type=F32)
    for e in range(rows.shape[0] // 16):
        for q in range(4):
            tall[e, pl.ds(q, 16, stride=4), :] = o[e*16:(e+1)*16, q*128:(q+1)*128]
    return [tall[e].astype(BF) for e in range(rows.shape[0] // 16)]


def halo_kernel(nx, ny, width, src, dst, own_table, buf, table, fan_ref, tall, load, store, send, recv):
    def taken(d, n):
        return {0: pl.ds(0, n), 1: pl.ds(n - width, width), -1: pl.ds(0, width)}[d]

    def landed(d, n):
        return {0: pl.ds(width, n), 1: pl.ds(0, width), -1: pl.ds(n + width, width)}[d]

    def message(s, dx, dy):
        return (0, dx, dy, lambda to: remote(src.at[taken(dx, nx), taken(dy, ny)], dst.at[landed(dx, nx), landed(dy, ny)], send.at[s], recv.at[s], to))

    messages = [message(s, dx, dy) for s, (dx, dy) in enumerate(SIDES)]
    greet()
    fill = pltpu.make_async_copy(src, buf, load.at[0])
    fill.start()
    fan_ref[...] = spread_lanes()
    meet()
    send_all(messages, 0)
    fill.wait()
    chunks = 4
    part = nx // chunks
    stores = []
    for c in range(chunks):
        def expand(i, carry):
            x = c*part + i
            for y, t in enumerate(expanded(buf[x].reshape(ny*16, 128), fan_ref, tall)):
                table[x, y] = t
            return carry
        lax.fori_loop(0, part, expand, 0)
        xs = pl.ds(c*part, part)
        stores.append(pltpu.make_async_copy(table.at[xs], own_table.at[xs], store.at[c]))
        stores[-1].start()
    wait_all(messages)
    for s in stores:
        s.wait()


def halo_call(src, dst_shape, width):
    anyspec = pl.BlockSpec(memory_space=pl.ANY)
    nx, ny = src.shape[:2]
    return pl.pallas_call(functools.partial(halo_kernel, nx, ny, width),
        in_specs=[anyspec], out_specs=[anyspec]*2, out_shape=[jax.ShapeDtypeStruct(dst_shape, src.dtype), jax.ShapeDtypeStruct((nx, ny, 64, 128), BF)],
        scratch_shapes=[pltpu.VMEM(src.shape, BF), pltpu.VMEM((nx, ny, 64, 128), BF), pltpu.VMEM((128, 512), BF), pltpu.VMEM((ny, 64, 128), F32),
                        pltpu.SemaphoreType.DMA((1,)), pltpu.SemaphoreType.DMA((4,)), pltpu.SemaphoreType.DMA((8,)), pltpu.SemaphoreType.DMA((8,))],
        compiler_params=pltpu.CompilerParams(vmem_limit_bytes=40<<20, collective_id=1, has_side_effects=True), name="halo")(src)


def pick_blocks(pieces, block):
    out = pieces[3]
    for b in (2, 1, 0):
        out = jnp.where(block == b, pieces[b], out)
    return out


def turn(v, s):
    s = s % 4
    return v if s == 0 else pltpu.roll(v, 32*s, 1)


def gram_rows(x, p_buf, z_buf, g_buf, low_buf, slot):
    block16 = lax.broadcasted_iota(jnp.int32, (16,128), 1)//32
    block8 = lax.broadcasted_iota(jnp.int32, (8,128), 1)//32
    for half in range(2):
        p = [p_buf[x, 4*half+b] for b in range(4)]
        yh = jnp.concatenate([pick_blocks([turn(p[b], b-q) for b in range(4)], block16) for q in range(4)], axis=0)
        hi = yh.astype(BF)
        lo = (yh - hi.astype(F32)).astype(BF)
        o = lax.dot_general(jnp.concatenate([hi, lo, hi], axis=0), jnp.concatenate([hi, hi, lo], axis=0), (((0,),(0,)),((),())), preferred_element_type=F32)
        r = [pick_blocks([o[32*b+8*kb:32*b+8*kb+8] for b in range(4)], block8) * (1.0/64) for kb in range(4)]
        for b in range(4):
            z_buf[slot, :, b, :] = pick_blocks([turn(r[kb], kb-b) for kb in range(4)], block8)
        z = z_buf[slot]
        zh = z.astype(BF)
        g_buf[half, :, x] = zh
        low_buf[half, :, x] = (z - zh.astype(F32)).astype(BF)


def gram_kernel(nx, chunks, with_halo, *refs):
    if with_halo:
        b_ref, tile, gpad, glow, tiles, p_buf, z_buf, g_buf, low_buf, load, store, send, recv = refs
    else:
        b_ref, gpad, glow, p_buf, z_buf, g_buf, low_buf, load, store = refs
    part = nx // chunks
    loads = [[pltpu.make_async_copy(b_ref.at[pl.ds(c*part, part), :, y], p_buf.at[pl.ds(c*part, part), y], load.at[c, y]) for y in range(8)] for c in range(chunks)]
    for group in loads:
        for c in group: c.start()
    messages = []
    if with_halo:
        def block(phase, dx, dy, sx, tx):
            sy = {0: pl.ds(0, 2), 1: pl.ds(1, 1), -1: pl.ds(0, 1)}[dy]
            ty = {0: pl.ds(1, 2), 1: pl.ds(0, 1), -1: pl.ds(3, 1)}[dy]
            s = len(messages)
            messages.append((phase, dx, dy, lambda to: remote(g_buf.at[sy, :, sx], gpad.at[ty, :, tx], send.at[s], recv.at[s], to)))
        def roots(dx, dy):
            s = len(messages)
            messages.append((0, dx, dy, lambda to: remote(tile, tiles.at[1-dx, 1-dy], send.at[s], recv.at[s], to)))
        for dx, dy in SIDES:
            roots(dx, dy)
        for dy in (-1, 0, 1):
            block(0, -1, dy, pl.ds(0, 4), pl.ds(nx+4, 4))
            block(chunks-1, 1, dy, pl.ds(nx-4, 4), pl.ds(0, 4))
        for c in range(chunks):
            for dy in (-1, 1):
                block(c, 0, dy, pl.ds(c*part, part), pl.ds(4 + c*part, part))
        greet()
    for c in range(chunks):
        for one in loads[c]: one.wait()
        def rows(i, carry):
            for u in range(2):
                gram_rows(c*part + 2*i + u, p_buf, z_buf, g_buf, low_buf, u)
            return carry
        lax.fori_loop(0, part//2, rows, 0)
        if with_halo:
            if c == 0:
                meet()
            send_all(messages, c)
    mine = [pltpu.make_async_copy(g_buf, gpad.at[pl.ds(1, 2), :, pl.ds(4, nx)], store.at[0]), pltpu.make_async_copy(low_buf, glow, store.at[1])]
    if with_halo:
        mine.append(pltpu.make_async_copy(tile, tiles.at[1, 1], store.at[2]))
    for c in mine: c.start()
    if with_halo:
        wait_all(messages)
    for c in mine: c.wait()


def gram_call(nn, tile=None, chunks=4):
    nx = nn.shape[0]
    anyspec = pl.BlockSpec(memory_space=pl.ANY)
    gshape = jax.ShapeDtypeStruct((4, 8, nx+8, 4, 128), BF)
    scratch = [pltpu.VMEM((nx,8,16,128),F32), pltpu.VMEM((2,8,4,128),F32), pltpu.VMEM((2,8,nx,4,128),BF), pltpu.VMEM((2,8,nx,4,128),BF),
               pltpu.SemaphoreType.DMA((chunks,8)), pltpu.SemaphoreType.DMA((3,))]
    lshape = jax.ShapeDtypeStruct((2, 8, nx, 4, 128), BF)
    kern = functools.partial(gram_kernel, nx, chunks, tile is not None)
    if tile is None:
        return pl.pallas_call(kern, in_specs=[anyspec], out_specs=[anyspec]*2, out_shape=[gshape, lshape], scratch_shapes=scratch,
            compiler_params=pltpu.CompilerParams(vmem_limit_bytes=56<<20), name="gram")(nn)
    return pl.pallas_call(kern, in_specs=[anyspec]*2, out_specs=[anyspec]*3,
        out_shape=[gshape, lshape, jax.ShapeDtypeStruct((3,3)+tile.shape, tile.dtype)],
        scratch_shapes=scratch + [pltpu.SemaphoreType.DMA((14 + 2*chunks,)), pltpu.SemaphoreType.DMA((14 + 2*chunks,))],
        compiler_params=pltpu.CompilerParams(vmem_limit_bytes=56<<20, collective_id=0, has_side_effects=True), name="gram")(nn, tile)


def local_slots(nx, ny):
    grid_y = ny * lax.axis_size("gy")
    first_x, first_y = lax.axis_index("gx")*nx - 2, lax.axis_index("gy")*ny - 2
    bits = grid_y.bit_length() - 1

    def place(flat):
        x = lax.shift_right_logical(flat, bits) if grid_y == 1 << bits else lax.div(flat, grid_y)
        return x - first_x, flat - x*grid_y - first_y
    return place


def factor_kernel(nx, cells_ref, root_ref, rid_ref, b_ref, g_ref, gl_ref, t_ref, tb_ref, comp, idcol, tab, bd, v_ref, g_buf, gl_buf, p_buf, t_buf, tb_buf, sem, load, store):
    ncell = cells_ref.shape[0]
    px = nx + 8
    gx, gy = lax.axis_index("gx"), lax.axis_index("gy")
    place = local_slots(nx, 8)
    els = rid_ref.shape[1]
    chunks = 4
    part = nx // chunks
    copies_g = [pltpu.make_async_copy(g_ref, g_buf, sem.at[0]), pltpu.make_async_copy(gl_ref, gl_buf, sem.at[1])]
    for c in copies_g: c.start()
    loads = [pltpu.make_async_copy(b_ref.at[:, :, y], p_buf.at[:, y], load.at[y]) for y in range(8)]
    for c in loads: c.start()
    def compact(i, n):
        cid = cells_ref[i]
        idcol[pl.ds(n, 1), :] = jnp.full((1, 128), cid, jnp.int32)
        comp[i] = n
        return n + (cid >= 0).astype(jnp.int32)
    n = lax.fori_loop(0, ncell, compact, 0, unroll=8)
    for c in copies_g: c.wait()
    @pl.when(gx == 0)
    def _(): g_buf[:, :, 0:16] = jnp.zeros((4, 8, 16, 128), BF)
    @pl.when(gx == lax.axis_size("gx") - 1)
    def _(): g_buf[:, :, 4*px-16:4*px] = jnp.zeros((4, 8, 16, 128), BF)
    @pl.when(gy == 0)
    def _(): g_buf[0] = jnp.zeros((8, 4*px, 128), BF)
    @pl.when(gy == lax.axis_size("gy") - 1)
    def _(): g_buf[3] = jnp.zeros((8, 4*px, 128), BF)

    sub = lax.broadcasted_iota(jnp.int32, (32, 128), 0)
    block = lax.broadcasted_iota(jnp.int32, (32, 128), 1)//32
    def batch(bi, c):
        base = bi*128
        ids = idcol[pl.ds(base, 128), :]
        hot = [jnp.where(ids == rid_ref[:, 128*t:128*t+128], 1.0, 0.0).astype(BF) for t in range(els//128)]
        hot = jnp.concatenate(hot, axis=1)
        for k8 in range(8):
            g = jnp.concatenate([g_buf[yb, k8] for yb in range(4)] + [gl_buf[yb, k8] for yb in range(2)], axis=0)
            s = jnp.dot(hot, g, preferred_element_type=F32).T
            for kb in range(4):
                v_ref[32*(8*kb+k8):32*(8*kb+k8)+32, :] = s[32*kb:32*kb+32]
        for jb in range(4):
            def pivot(j8, c2):
                j = jb*8 + j8
                row = v_ref[pl.ds(pl.multiple_of(j*32, 32), 32), :]
                d = lax.rsqrt(v_ref[pl.ds(j*33, 1), :])
                at_j = sub == j
                u = jnp.where(at_j, d, row*d)
                v_ref[pl.ds(pl.multiple_of(j*32, 32), 32), :] = u
                for i in range(jb*8, 32):
                    f = u[i:i+1, :]
                    old = v_ref[32*i:32*i+32, :]
                    if i < jb*8+8:
                        later = i > j
                        f = jnp.where(later, f, 0.0)
                        new = jnp.where(at_j & later, 0.0, old) - f*u
                        new = jnp.where(later, new, old)
                    else:
                        new = jnp.where(at_j, 0.0, old) - f*u
                    v_ref[32*i:32*i+32, :] = new
                return c2
            lax.fori_loop(0, 8, pivot, 0)
        for k in range(32):
            m = v_ref[pl.ds(k, 32, stride=32), :]
            m = jnp.where(sub >= k, m, 0.0)
            tab[k] = jnp.concatenate([m]*4, axis=0).T
        def spread(i, c2):
            for u in range(4):
                r = 4*i + u
                w = tab[:, pl.ds(r, 1), :].reshape(32, 128)
                hi = w.astype(BF).astype(F32)
                lo = w - hi
                bd[base + r, 0:128, :] = jnp.concatenate([jnp.where(block == q, hi, 0.0) for q in range(4)], axis=0).astype(BF)
                bd[base + r, 128:256, :] = jnp.concatenate([jnp.where(block == q, lo, 0.0) for q in range(4)], axis=0).astype(BF)
            return c2
        lax.fori_loop(0, (jnp.minimum(n - base, 128) + 3)//4, spread, 0)
        return c
    lax.fori_loop(0, (n + 127)//128, batch, 0)

    for c in loads: c.wait()
    stores = []
    for ch in range(chunks):
        def one_x(i, c):
            x = ch*part + i
            for y in range(8):
                rx, ry = place(root_ref[y, x])
                r = comp[rx*12 + ry]
                p = p_buf[x, y]
                ph = p.astype(BF)
                plo = (p - ph.astype(F32)).astype(BF)
                lhs = jnp.concatenate([jnp.concatenate([ph, ph], axis=1), jnp.concatenate([plo, jnp.zeros_like(plo)], axis=1)], axis=0)
                o = jnp.dot(lhs, bd[r], preferred_element_type=F32)
                t = o[:16] + o[16:]
                t_buf[x, y] = t
                tb_buf[x, y] = t.astype(BF)
            return c
        lax.fori_loop(0, part, one_x, 0)
        xs = pl.ds(ch*part, part)
        for c in (pltpu.make_async_copy(t_buf.at[xs], t_ref.at[xs], store.at[0, ch]), pltpu.make_async_copy(tb_buf.at[xs], tb_ref.at[xs], store.at[1, ch])):
            c.start()
            stores.append(c)
    for c in stores: c.wait()


def factor_call(cells, roots, rid, nn, gpad, glow):
    nx = nn.shape[0]
    anyspec = pl.BlockSpec(memory_space=pl.ANY)
    nc = (nx+4)*12
    ncp = (nc + 127)//128*128
    return pl.pallas_call(functools.partial(factor_kernel, nx),
        grid_spec=pltpu.PrefetchScalarGridSpec(num_scalar_prefetch=2, grid=(1,),
          in_specs=[pl.BlockSpec(rid.shape, lambda i,*_: (0,0)), anyspec, anyspec, anyspec],
          out_specs=[anyspec, anyspec],
          scratch_shapes=[pltpu.SMEM((nc,), jnp.int32), pltpu.VMEM((ncp+128,128), jnp.int32), pltpu.VMEM((32,128,128),F32), pltpu.VMEM((ncp,256,128),BF),
             pltpu.VMEM((1024,128),F32), pltpu.VMEM(gpad.shape,BF), pltpu.VMEM(glow.shape,BF), pltpu.VMEM((nx,8,16,128),F32), pltpu.VMEM((nx,8,16,128),F32), pltpu.VMEM((nx,8,16,128),BF),
             pltpu.SemaphoreType.DMA((2,)), pltpu.SemaphoreType.DMA((8,)), pltpu.SemaphoreType.DMA((2,4))]),
        out_shape=[jax.ShapeDtypeStruct((nx,8,16,128),F32), jax.ShapeDtypeStruct((nx,8,16,128),BF)],
        compiler_params=pltpu.CompilerParams(vmem_limit_bytes=62<<20), name="factor")(cells, roots, rid, nn, gpad, glow)


def apply_kernel(nx, px, py, xb, idx_ref, t_ref, d_ref, own_ref, tp_ref, a_ref, out_ref, abuf, table, wide, tall, fan_ref, scale_ref, tbuf, obuf, sems, osem, tsem):
    step = pl.program_id(0)
    steps = nx // xb
    slot = lax.rem(step, 2)
    def fetch(s, slot):
        for c in range(32):
            for kp in range(2):
                pltpu.make_async_copy(a_ref.at[pl.ds(s*xb, xb), :, c, pl.ds(2*kp, 2), :], abuf.at[slot, :, :, kp, pl.ds(32*(c % 2) + 2*(c//2), 2), :], sems.at[slot]).start()
    def outs(s, slot):
        return [pltpu.make_async_copy(obuf.at[slot, :, y], out_ref.at[pl.ds(s*xb, xb), :, y], osem.at[slot, y]) for y in range(8)]
    lane = lax.broadcasted_iota(jnp.int32, (16, 128), 1)
    place = local_slots(nx, 8)
    def load_at(flat):
        tx, ty = place(flat)
        return table[tx, ty]
    @pl.when(step == 0)
    def _():
        strips = [(pl.ds(0, 2), pl.ds(0, py)), (pl.ds(px-2, 2), pl.ds(0, py)), (pl.ds(2, nx), pl.ds(0, 2)), (pl.ds(2, nx), pl.ds(py-2, 2))]
        fill = [pltpu.make_async_copy(tp_ref.at[sx, sy], tbuf.at[sx, sy], tsem.at[i]) for i, (sx, sy) in enumerate(strips)]
        own = pltpu.make_async_copy(own_ref, table.at[pl.ds(2, nx), pl.ds(2, py-4)], tsem.at[4])
        for c in fill: c.start()
        own.start()
        fetch(0, 0)
        fan_ref[...] = spread_lanes()
        for c in fill: c.wait()
        def ends(i, carry):
            x = jnp.where(i < 2, i, px - 4 + i)
            for y, t in enumerate(expanded(tbuf[x].reshape(py*16, 128), fan_ref, tall)):
                table[x, y] = t
            return carry
        lax.fori_loop(0, 4, ends, 0)
        def sides(i, carry):
            at = [(2 + 3*i + u, y) for u in range(3) for y in (0, 1, py-2, py-1)]
            rows = jnp.concatenate([tbuf[x, y] for x, y in at], axis=0)
            for (x, y), t in zip(at, expanded(rows, fan_ref, tall)):
                table[x, y] = t
            return carry
        lax.fori_loop(0, nx//3, sides, 0)
        own.wait()
    @pl.when(step + 1 < steps)
    def _():
        fetch(step+1, 1-slot)
    @pl.when(step >= 2)
    def _():
        for c in outs(step-2, slot): c.wait()
    pltpu.make_async_copy(abuf.at[slot], abuf.at[slot], sems.at[slot]).wait()
    row16 = lax.broadcasted_iota(jnp.int32, (16, 128), 0)
    col4 = (lax.broadcasted_iota(jnp.int32, (16, 128), 1) % 64) // 4
    pick = (lax.broadcasted_iota(jnp.int32, (64, 128), 0) % 4 == lax.broadcasted_iota(jnp.int32, (64, 128), 1) // 32)
    pick = jnp.where(pick, 1.0, 0.0).astype(BF)
    pick = jnp.concatenate([pick, pick], axis=0)
    lanew = lax.broadcasted_iota(jnp.int32, (64, 128), 1)
    def one_x(xi, carry):
        d = d_ref[xi] * OMEGA
        hi = d.astype(BF).astype(F32)
        both = jnp.concatenate([hi, d - hi], axis=1)
        spread = jnp.concatenate([jnp.where(row16 == col4, both[y:y+1], 0.0) for y in range(8)], axis=0)
        scale_ref[...] = jnp.dot(spread.astype(BF), pick, preferred_element_type=F32)
        for y in range(8):
            x = step*xb + xi
            parts = []
            for kp in range(2):
                t0 = load_at(idx_ref[y, 2*kp, x])
                t1 = load_at(idx_ref[y, 2*kp+1, x])
                r = jnp.where(lanew < 64, t0, t1)
                parts.append(jnp.where((lanew//32) % 2 == 0, r, jnp.zeros_like(r)))
                parts.append(jnp.where((lanew//32) % 2 == 1, r, jnp.zeros_like(r)))
            rhs = jnp.concatenate(parts, axis=0)
            lhs = jnp.concatenate([abuf[slot, xi, y, 0], abuf[slot, xi, y, 1]], axis=1)
            wide[y] = jnp.dot(lhs, rhs, preferred_element_type=F32)
        for y in range(8):
            r = [[wide[y, pl.ds(32*ch+p, 16, stride=2), :] for p in range(2)] for ch in range(2)]
            u = jnp.where(lane < 64, r[0][0], r[1][1]) + pltpu.roll(jnp.where(lane < 64, r[1][0], r[0][1]), 64, 1)
            obuf[slot, xi, y] = t_ref[xi, y] - scale_ref[16*y:16*y+16, :] * u
        return carry
    lax.fori_loop(0, xb, one_x, 0)
    for c in outs(step, slot): c.start()
    @pl.when(step == steps - 1)
    def _():
        for c in outs(step-1, 1-slot) + outs(step, slot): c.wait()


def apply_call(idx, t4, d, own, tp, a6, xb=12):
    nx = t4.shape[0]; px, py = tp.shape[:2]
    anyspec = pl.BlockSpec(memory_space=pl.ANY)
    return pl.pallas_call(functools.partial(apply_kernel, nx, px, py, xb),
        grid_spec=pltpu.PrefetchScalarGridSpec(num_scalar_prefetch=1, grid=(nx//xb,),
          in_specs=[pl.BlockSpec((xb,8,16,128), lambda i,*_:(i,0,0,0)), pl.BlockSpec((xb,8,64), lambda i,*_:(i,0,0)),
                    anyspec, anyspec, anyspec],
          out_specs=anyspec,
          scratch_shapes=[pltpu.VMEM((2,xb,8,2,64,128),BF), pltpu.VMEM((px,py,64,128),BF), pltpu.VMEM((8,64,128),F32), pltpu.VMEM((12,64,128),F32), pltpu.VMEM((128,512),BF), pltpu.VMEM((128,128),F32),
             pltpu.VMEM((px,py,16,128),BF), pltpu.VMEM((2,xb,8,16,128),F32), pltpu.SemaphoreType.DMA((2,)), pltpu.SemaphoreType.DMA((2,8)), pltpu.SemaphoreType.DMA((5,))]),
        out_shape=jax.ShapeDtypeStruct((nx,16,8,128),F32),
        compiler_params=pltpu.CompilerParams(vmem_limit_bytes=56<<20), name="apply")(idx, t4, d, own, tp, a6)


def body(near_null, a_blocks, inv_diag, root_map, neighbours):
    nx, ny = root_map.shape
    grid_x, grid_y = nx * lax.axis_size("gx"), ny * lax.axis_size("gy")
    gx, gy = lax.axis_index("gx"), lax.axis_index("gy")
    sx, sy = gx * nx, gy * ny
    nn = near_null.reshape(nx, ny, 16, 128).transpose(0, 2, 1, 3)
    a5 = a_blocks.reshape(nx, ny, 4, 32, 128).transpose(0, 1, 3, 2, 4)
    roots = root_map.T
    gpad, glow, tiles = gram_call(nn, roots)
    around = tiles.transpose(0, 3, 1, 2).reshape(3 * nx, 3 * ny)[nx - 4:2 * nx + 4, ny - 4:2 * ny + 4]
    ax = sx - 4 + jnp.arange(nx + 8, dtype=jnp.int32)[:, None]
    ay = sy - 4 + jnp.arange(ny + 8, dtype=jnp.int32)[None, :]
    around = jnp.where((ax >= 0) & (ax < grid_x) & (ay >= 0) & (ay < grid_y), around, -1)
    cells = jnp.where(around == ax * grid_y + ay, around, -1)[2:-2, 2:-2].reshape(-1)
    rid = jnp.concatenate([around.reshape(nx + 8, 4, 4).transpose(1, 0, 2).reshape(1, -1), root_map.reshape(nx, 2, 4).transpose(1, 0, 2).reshape(1, -1)], axis=1)
    tent, low = factor_call(cells, roots, rid, nn, gpad.reshape(4, 8, -1, 128), glow.reshape(2, 8, -1, 128))
    low_pad, own_table = halo_call(low, (nx + 4, ny + 4, 16, 128), 2)
    out = apply_call(neighbours.transpose(1, 2, 0), tent, inv_diag, own_table, low_pad, a5)
    return out.transpose(0, 2, 1, 3).reshape(nx, ny, 2048)


def solution(mesh):
    in_specs = (P("gx", "gy", None), P("gx", "gy", None, None), P("gx", "gy", None), P("gx", "gy"), P("gx", "gy", None))
    return jax.shard_map(body, mesh=mesh, in_specs=in_specs, out_specs=P("gx", "gy", None), check_vma=False)
```

```python
import functools

import jax
import jax.numpy as jnp
from jax import lax
from jax.experimental import pallas as pl
from jax.experimental.pallas import tpu as pltpu
from jax.sharding import PartitionSpec as P

F32 = jnp.float32
BF = jnp.bfloat16
OMEGA = 2.0 / 3.0

SIDES = [(dx, dy) for dx in (-1, 0, 1) for dy in (-1, 0, 1) if dx or dy]


def there(dx, dy):
    gx, gy = lax.axis_index("gx"), lax.axis_index("gy")
    ok = jnp.bool_(True)
    if dx:
        ok &= (gx + dx >= 0) & (gx + dx < lax.axis_size("gx"))
    if dy:
        ok &= (gy + dy >= 0) & (gy + dy < lax.axis_size("gy"))
    return ok


def peer(dx, dy):
    return (lax.axis_index("gx") + dx, lax.axis_index("gy") + dy)


def remote(src, dst, send, recv, to):
    return pltpu.make_async_remote_copy(src_ref=src, dst_ref=dst, send_sem=send, recv_sem=recv, device_id=to, device_id_type=pl.DeviceIdType.MESH)


def greet():
    for dx, dy in SIDES:
        @pl.when(there(dx, dy))
        def _():
            pl.semaphore_signal(pltpu.get_barrier_semaphore(), inc=1, device_id=peer(dx, dy), device_id_type=pl.DeviceIdType.MESH)


def meet():
    gx, gy = lax.axis_index("gx"), lax.axis_index("gy")
    wide = 1 + (gx > 0).astype(jnp.int32) + (gx < lax.axis_size("gx") - 1).astype(jnp.int32)
    tall = 1 + (gy > 0).astype(jnp.int32) + (gy < lax.axis_size("gy") - 1).astype(jnp.int32)
    pl.semaphore_wait(pltpu.get_barrier_semaphore(), wide * tall - 1)


def send_all(messages, phase):
    for at, dx, dy, copy in messages:
        if at == phase:
            @pl.when(there(dx, dy))
            def _():
                copy(peer(dx, dy)).start()


def wait_all(messages):
    for _, dx, dy, copy in messages:
        @pl.when(there(-dx, -dy))
        def _():
            copy(peer(dx, dy)).wait_recv()
    for _, dx, dy, copy in messages:
        @pl.when(there(dx, dy))
        def _():
            copy(peer(dx, dy)).wait_send()


def spread_lanes():
    r = lax.broadcasted_iota(jnp.int32, (128, 512), 0)
    c = lax.broadcasted_iota(jnp.int32, (128, 512), 1)
    return jnp.where((r // 32 == c // 128) & (r % 32 == c % 32), 1.0, 0.0).astype(BF)


def expanded(rows, fan_ref, tall):
    o = jnp.dot(rows, fan_ref[...], preferred_element_type=F32)
    for e in range(rows.shape[0] // 16):
        for q in range(4):
            tall[e, pl.ds(q, 16, stride=4), :] = o[e*16:(e+1)*16, q*128:(q+1)*128]
    return [tall[e].astype(BF) for e in range(rows.shape[0] // 16)]


def halo_kernel(nx, ny, width, src, dst, own_table, buf, table, fan_ref, tall, load, store, send, recv):
    def taken(d, n):
        return {0: pl.ds(0, n), 1: pl.ds(n - width, width), -1: pl.ds(0, width)}[d]

    def landed(d, n):
        return {0: pl.ds(width, n), 1: pl.ds(0, width), -1: pl.ds(n + width, width)}[d]

    def message(s, dx, dy):
        return (0, dx, dy, lambda to: remote(src.at[taken(dx, nx), taken(dy, ny)], dst.at[landed(dx, nx), landed(dy, ny)], send.at[s], recv.at[s], to))

    messages = [message(s, dx, dy) for s, (dx, dy) in enumerate(SIDES)]
    greet()
    fill = pltpu.make_async_copy(src, buf, load.at[0])
    fill.start()
    fan_ref[...] = spread_lanes()
    meet()
    send_all(messages, 0)
    fill.wait()
    chunks = 4
    part = nx // chunks
    stores = []
    for c in range(chunks):
        def expand(i, carry):
            x = c*part + i
            for y, t in enumerate(expanded(buf[x].reshape(ny*16, 128), fan_ref, tall)):
                table[x, y] = t
            return carry
        lax.fori_loop(0, part, expand, 0)
        xs = pl.ds(c*part, part)
        stores.append(pltpu.make_async_copy(table.at[xs], own_table.at[xs], store.at[c]))
        stores[-1].start()
    wait_all(messages)
    for s in stores:
        s.wait()


def halo_call(src, dst_shape, width):
    anyspec = pl.BlockSpec(memory_space=pl.ANY)
    nx, ny = src.shape[:2]
    return pl.pallas_call(functools.partial(halo_kernel, nx, ny, width),
        in_specs=[anyspec], out_specs=[anyspec]*2, out_shape=[jax.ShapeDtypeStruct(dst_shape, src.dtype), jax.ShapeDtypeStruct((nx, ny, 64, 128), BF)],
        scratch_shapes=[pltpu.VMEM(src.shape, BF), pltpu.VMEM((nx, ny, 64, 128), BF), pltpu.VMEM((128, 512), BF), pltpu.VMEM((ny, 64, 128), F32),
                        pltpu.SemaphoreType.DMA((1,)), pltpu.SemaphoreType.DMA((4,)), pltpu.SemaphoreType.DMA((8,)), pltpu.SemaphoreType.DMA((8,))],
        compiler_params=pltpu.CompilerParams(vmem_limit_bytes=62<<20, collective_id=1, has_side_effects=True), name="halo")(src)


UNROLL = 6


def pick_blocks(pieces, block):
    out = pieces[3]
    for b in (2, 1, 0):
        out = jnp.where(block == b, pieces[b], out)
    return out


def transpose_blocks(p, lane):
    block = lane >> 5
    return [pick_blocks([p[b] if b == q else pltpu.roll(p[b], 32*((b-q) % 4), 1) for b in range(4)], block) for q in range(4)]


def gram_rows(xs, p_buf, z_buf, g_buf, low_buf):
    lane16 = lax.broadcasted_iota(jnp.int32, (16,128), 1)
    lane8 = lax.broadcasted_iota(jnp.int32, (8,128), 1)
    block8 = lane8//32
    work = [(x, half) for x in xs for half in range(2)]
    outs = []
    for x, half in work:
        yh = jnp.concatenate(transpose_blocks([p_buf[x, 4*half+b] for b in range(4)], lane16), axis=0)
        hi = yh.astype(BF)
        lo = (yh - hi.astype(F32)).astype(BF)
        outs.append(lax.dot_general(jnp.concatenate([hi, lo, hi], axis=0), jnp.concatenate([hi, hi, lo], axis=0), (((0,),(0,)),((),())), preferred_element_type=F32))
    for slot, o in enumerate(outs):
        r = [pick_blocks([o[32*b+8*kb:32*b+8*kb+8] for b in range(4)], block8) * (1.0/64) for kb in range(4)]
        for b, g in enumerate(transpose_blocks(r, lane8)):
            z_buf[slot, pl.ds(b, 8, stride=4), :] = g
    for slot, (x, half) in enumerate(work):
        z = z_buf[slot]
        zh = z.astype(BF)
        g_buf[half, :, x] = zh.reshape(8,4,128)
        low_buf[half, :, x] = (z - zh.astype(F32)).astype(BF).reshape(8,4,128)


def gram_kernel(nx, chunks, with_halo, *refs):
    if with_halo:
        b_ref, tile, gpad, glow, tiles, p_buf, z_buf, g_buf, low_buf, load, store, send, recv = refs
    else:
        b_ref, gpad, glow, p_buf, z_buf, g_buf, low_buf, load, store = refs
    part = nx // chunks
    loads = [[pltpu.make_async_copy(b_ref.at[pl.ds(c*part, part), :, y], p_buf.at[pl.ds(c*part, part), y], load.at[c, y]) for y in range(8)] for c in range(chunks)]
    for group in loads:
        for c in group: c.start()
    messages = []
    if with_halo:
        def block(phase, dx, dy, sx, tx):
            sy = {0: pl.ds(0, 2), 1: pl.ds(1, 1), -1: pl.ds(0, 1)}[dy]
            ty = {0: pl.ds(1, 2), 1: pl.ds(0, 1), -1: pl.ds(3, 1)}[dy]
            s = len(messages)
            messages.append((phase, dx, dy, lambda to: remote(g_buf.at[sy, :, sx], gpad.at[ty, :, tx], send.at[s], recv.at[s], to)))
        def roots(dx, dy):
            s = len(messages)
            messages.append((0, dx, dy, lambda to: remote(tile, tiles.at[1-dx, 1-dy], send.at[s], recv.at[s], to)))
        for dx, dy in SIDES:
            roots(dx, dy)
        for dy in (-1, 0, 1):
            block(0, -1, dy, pl.ds(0, 4), pl.ds(nx+4, 4))
            block(chunks-1, 1, dy, pl.ds(nx-4, 4), pl.ds(0, 4))
        for c in range(chunks):
            for dy in (-1, 1):
                block(c, 0, dy, pl.ds(c*part, part), pl.ds(4 + c*part, part))
        greet()
    for c in range(chunks):
        for one in loads[c]: one.wait()
        def rows(i, carry):
            gram_rows([c*part + UNROLL*i + u for u in range(UNROLL)], p_buf, z_buf, g_buf, low_buf)
            return carry
        lax.fori_loop(0, part//UNROLL, rows, 0)
        if with_halo:
            if c == 0:
                meet()
            send_all(messages, c)
    mine = [pltpu.make_async_copy(g_buf, gpad.at[pl.ds(1, 2), :, pl.ds(4, nx)], store.at[0]), pltpu.make_async_copy(low_buf, glow, store.at[1])]
    if with_halo:
        mine.append(pltpu.make_async_copy(tile, tiles.at[1, 1], store.at[2]))
    for c in mine: c.start()
    if with_halo:
        wait_all(messages)
    for c in mine: c.wait()


def gram_call(nn, tile=None, chunks=4):
    nx = nn.shape[0]
    anyspec = pl.BlockSpec(memory_space=pl.ANY)
    gshape = jax.ShapeDtypeStruct((4, 8, nx+8, 4, 128), BF)
    scratch = [pltpu.VMEM((nx,8,16,128),F32), pltpu.VMEM((2*UNROLL,32,128),F32), pltpu.VMEM((2,8,nx,4,128),BF), pltpu.VMEM((2,8,nx,4,128),BF),
               pltpu.SemaphoreType.DMA((chunks,8)), pltpu.SemaphoreType.DMA((3,))]
    lshape = jax.ShapeDtypeStruct((2, 8, nx, 4, 128), BF)
    kern = functools.partial(gram_kernel, nx, chunks, tile is not None)
    if tile is None:
        return pl.pallas_call(kern, in_specs=[anyspec], out_specs=[anyspec]*2, out_shape=[gshape, lshape], scratch_shapes=scratch,
            compiler_params=pltpu.CompilerParams(vmem_limit_bytes=62<<20), name="gram")(nn)
    return pl.pallas_call(kern, in_specs=[anyspec]*2, out_specs=[anyspec]*3,
        out_shape=[gshape, lshape, jax.ShapeDtypeStruct((3,3)+tile.shape, tile.dtype)],
        scratch_shapes=scratch + [pltpu.SemaphoreType.DMA((14 + 2*chunks,)), pltpu.SemaphoreType.DMA((14 + 2*chunks,))],
        compiler_params=pltpu.CompilerParams(vmem_limit_bytes=62<<20, collective_id=0, has_side_effects=True), name="gram")(nn, tile)


FACTOR_UNROLL = 4


def local_slots(nx, ny):
    grid_y = ny * lax.axis_size("gy")
    first_x, first_y = lax.axis_index("gx")*nx - 2, lax.axis_index("gy")*ny - 2
    bits = grid_y.bit_length() - 1

    def place(flat):
        x = lax.shift_right_logical(flat, bits) if grid_y == 1 << bits else lax.div(flat, grid_y)
        return x - first_x, flat - x*grid_y - first_y
    return place


def factor_kernel(nx, cells_ref, root_ref, rid_ref, b_ref, g_ref, gl_ref, t_ref, tb_ref, comp, idcol, tab, bd, v_ref, g_buf, gl_buf, p_buf, t_buf, tb_buf, sem, load, store):
    ncell = cells_ref.shape[0]
    px = nx + 8
    gx, gy = lax.axis_index("gx"), lax.axis_index("gy")
    place = local_slots(nx, 8)
    els = rid_ref.shape[1]
    chunks = 4
    part = nx // chunks
    copies_g = [pltpu.make_async_copy(g_ref, g_buf, sem.at[0]), pltpu.make_async_copy(gl_ref, gl_buf, sem.at[1])]
    for c in copies_g: c.start()
    loads = [pltpu.make_async_copy(b_ref.at[:, :, y], p_buf.at[:, y], load.at[y]) for y in range(8)]
    for c in loads: c.start()
    def compact(i, n):
        cid = cells_ref[i]
        idcol[pl.ds(n, 1), :] = jnp.full((1, 128), cid, jnp.int32)
        comp[i] = n
        return n + (cid >= 0).astype(jnp.int32)
    n = lax.fori_loop(0, ncell, compact, 0, unroll=8)
    for c in copies_g: c.wait()
    @pl.when(gx == 0)
    def _(): g_buf[:, :, 0:16] = jnp.zeros((4, 8, 16, 128), BF)
    @pl.when(gx == lax.axis_size("gx") - 1)
    def _(): g_buf[:, :, 4*px-16:4*px] = jnp.zeros((4, 8, 16, 128), BF)
    @pl.when(gy == 0)
    def _(): g_buf[0] = jnp.zeros((8, 4*px, 128), BF)
    @pl.when(gy == lax.axis_size("gy") - 1)
    def _(): g_buf[3] = jnp.zeros((8, 4*px, 128), BF)

    sub = lax.broadcasted_iota(jnp.int32, (32, 128), 0)
    block = lax.broadcasted_iota(jnp.int32, (32, 128), 1)//32
    def batch(bi, c):
        base = bi*128
        ids = idcol[pl.ds(base, 128), :]
        hot = [jnp.where(ids == rid_ref[:, 128*t:128*t+128], 1.0, 0.0).astype(BF) for t in range(els//128)]
        hot = jnp.concatenate(hot, axis=1)
        for k8 in range(8):
            g = jnp.concatenate([g_buf[yb, k8] for yb in range(4)] + [gl_buf[yb, k8] for yb in range(2)], axis=0)
            s = jnp.dot(hot, g, preferred_element_type=F32).T
            for kb in range(4):
                v_ref[32*(8*kb+k8):32*(8*kb+k8)+32, :] = s[32*kb:32*kb+32]
        for jb in range(4):
            def pivot(j8, c2):
                j = jb*8 + j8
                row = v_ref[pl.ds(pl.multiple_of(j*32, 32), 32), :]
                d = lax.rsqrt(v_ref[pl.ds(j*33, 1), :])
                at_j = sub == j
                u = jnp.where(at_j, d, row*d)
                v_ref[pl.ds(pl.multiple_of(j*32, 32), 32), :] = u
                for i in range(jb*8, 32):
                    f = u[i:i+1, :]
                    old = v_ref[32*i:32*i+32, :]
                    if i < jb*8+8:
                        later = i > j
                        f = jnp.where(later, f, 0.0)
                        new = jnp.where(at_j & later, 0.0, old) - f*u
                        new = jnp.where(later, new, old)
                    else:
                        new = jnp.where(at_j, 0.0, old) - f*u
                    v_ref[32*i:32*i+32, :] = new
                return c2
            lax.fori_loop(0, 8, pivot, 0)
        for k in range(32):
            m = v_ref[pl.ds(k, 32, stride=32), :]
            m = jnp.where(sub >= k, m, 0.0)
            tab[k] = jnp.concatenate([m]*4, axis=0).T
        def spread(i, c2):
            for u in range(4):
                r = 4*i + u
                w = tab[:, pl.ds(r, 1), :].reshape(32, 128)
                hi = w.astype(BF).astype(F32)
                lo = w - hi
                bd[base + r, 0:128, :] = jnp.concatenate([jnp.where(block == q, hi, 0.0) for q in range(4)], axis=0).astype(BF)
                bd[base + r, 128:256, :] = jnp.concatenate([jnp.where(block == q, lo, 0.0) for q in range(4)], axis=0).astype(BF)
            return c2
        lax.fori_loop(0, (jnp.minimum(n - base, 128) + 3)//4, spread, 0)
        return c
    lax.fori_loop(0, (n + 127)//128, batch, 0)

    for c in loads: c.wait()
    stores = []
    for ch in range(chunks):
        def rows(i, c):
            at = [(ch*part + FACTOR_UNROLL*i + u, y) for u in range(FACTOR_UNROLL) for y in range(8)]
            outs = []
            for x, y in at:
                rx, ry = place(root_ref[y, x])
                r = comp[rx*12 + ry]
                p = p_buf[x, y]
                ph = p.astype(BF)
                plo = (p - ph.astype(F32)).astype(BF)
                lhs = jnp.concatenate([jnp.concatenate([ph, ph], axis=1), jnp.concatenate([plo, jnp.zeros_like(plo)], axis=1)], axis=0)
                outs.append(jnp.dot(lhs, bd[r], preferred_element_type=F32))
            for (x, y), o in zip(at, outs):
                t = o[:16] + o[16:]
                t_buf[x, y] = t
                tb_buf[x, y] = t.astype(BF)
            return c
        lax.fori_loop(0, part//FACTOR_UNROLL, rows, 0)
        xs = pl.ds(ch*part, part)
        for c in (pltpu.make_async_copy(t_buf.at[xs], t_ref.at[xs], store.at[0, ch]), pltpu.make_async_copy(tb_buf.at[xs], tb_ref.at[xs], store.at[1, ch])):
            c.start()
            stores.append(c)
    for c in stores: c.wait()


def factor_call(cells, roots, rid, nn, gpad, glow):
    nx = nn.shape[0]
    anyspec = pl.BlockSpec(memory_space=pl.ANY)
    nc = (nx+4)*12
    ncp = (nc + 127)//128*128
    return pl.pallas_call(functools.partial(factor_kernel, nx),
        grid_spec=pltpu.PrefetchScalarGridSpec(num_scalar_prefetch=2, grid=(1,),
          in_specs=[pl.BlockSpec(rid.shape, lambda i,*_: (0,0)), anyspec, anyspec, anyspec],
          out_specs=[anyspec, anyspec],
          scratch_shapes=[pltpu.SMEM((nc,), jnp.int32), pltpu.VMEM((ncp+128,128), jnp.int32), pltpu.VMEM((32,128,128),F32), pltpu.VMEM((ncp,256,128),BF),
             pltpu.VMEM((1024,128),F32), pltpu.VMEM(gpad.shape,BF), pltpu.VMEM(glow.shape,BF), pltpu.VMEM((nx,8,16,128),F32), pltpu.VMEM((nx,8,16,128),F32), pltpu.VMEM((nx,8,16,128),BF),
             pltpu.SemaphoreType.DMA((2,)), pltpu.SemaphoreType.DMA((8,)), pltpu.SemaphoreType.DMA((2,4))]),
        out_shape=[jax.ShapeDtypeStruct((nx,8,16,128),F32), jax.ShapeDtypeStruct((nx,8,16,128),BF)],
        compiler_params=pltpu.CompilerParams(vmem_limit_bytes=62<<20), name="factor")(cells, roots, rid, nn, gpad, glow)


APPLY_UNROLL = 4


def apply_kernel(nx, px, py, xb, idx_ref, t_ref, d_ref, own_ref, tp_ref, a_ref, out_ref, abuf, table, wide, tall, fan_ref, pick_ref, scale_ref, tbuf, obuf, sems, osem, tsem):
    step = pl.program_id(0)
    steps = nx // xb
    slot = lax.rem(step, 2)
    def fetch(s, slot):
        for c in range(32):
            for kp in range(2):
                pltpu.make_async_copy(a_ref.at[pl.ds(s*xb, xb), :, c, pl.ds(2*kp, 2), :], abuf.at[slot, :, :, kp, pl.ds(32*(c % 2) + 2*(c//2), 2), :], sems.at[slot]).start()
    def outs(s, slot):
        return [pltpu.make_async_copy(obuf.at[slot, :, y], out_ref.at[pl.ds(s*xb, xb), :, y], osem.at[slot, y]) for y in range(8)]
    lane = lax.broadcasted_iota(jnp.int32, (16, 128), 1)
    place = local_slots(nx, 8)
    def load_at(flat):
        tx, ty = place(flat)
        return table[tx, ty]
    @pl.when(step == 0)
    def _():
        strips = [(pl.ds(0, 2), pl.ds(0, py)), (pl.ds(px-2, 2), pl.ds(0, py)), (pl.ds(2, nx), pl.ds(0, 2)), (pl.ds(2, nx), pl.ds(py-2, 2))]
        fill = [pltpu.make_async_copy(tp_ref.at[sx, sy], tbuf.at[sx, sy], tsem.at[i]) for i, (sx, sy) in enumerate(strips)]
        own = pltpu.make_async_copy(own_ref, table.at[pl.ds(2, nx), pl.ds(2, py-4)], tsem.at[4])
        for c in fill: c.start()
        own.start()
        fetch(0, 0)
        fan_ref[...] = spread_lanes()
        pick_ref[...] = jnp.where((lax.broadcasted_iota(jnp.int32, (128, 128), 0) & 3) == lax.broadcasted_iota(jnp.int32, (128, 128), 1) >> 5, 1.0, 0.0).astype(BF)
        for c in fill: c.wait()
        def ends(i, carry):
            x = jnp.where(i < 2, i, px - 4 + i)
            for y, t in enumerate(expanded(tbuf[x].reshape(py*16, 128), fan_ref, tall)):
                table[x, y] = t
            return carry
        lax.fori_loop(0, 4, ends, 0)
        def sides(i, carry):
            at = [(2 + 3*i + u, y) for u in range(3) for y in (0, 1, py-2, py-1)]
            rows = jnp.concatenate([tbuf[x, y] for x, y in at], axis=0)
            for (x, y), t in zip(at, expanded(rows, fan_ref, tall)):
                table[x, y] = t
            return carry
        lax.fori_loop(0, nx//3, sides, 0)
        own.wait()
    @pl.when(step + 1 < steps)
    def _():
        fetch(step+1, 1-slot)
    @pl.when(step >= 2)
    def _():
        for c in outs(step-2, slot): c.wait()
    pltpu.make_async_copy(abuf.at[slot], abuf.at[slot], sems.at[slot]).wait()
    diagonal = (lax.broadcasted_iota(jnp.int32, (16, 128), 1) & 63) >> 2 == lax.broadcasted_iota(jnp.int32, (16, 128), 0)
    lanew = lax.broadcasted_iota(jnp.int32, (64, 128), 1)
    even = (lanew & 32) == 0
    left = lanew < 64
    zero = jnp.zeros((64, 128), BF)
    def some_rows(i, carry):
        xis = [APPLY_UNROLL*i + u for u in range(APPLY_UNROLL)]
        for u, xi in enumerate(xis):
            d = d_ref[xi] * OMEGA
            hi = d.astype(BF).astype(F32)
            both = jnp.concatenate([hi, d - hi], axis=1)
            spread = jnp.concatenate([jnp.where(diagonal, both[y:y+1], 0.0) for y in range(8)], axis=0)
            scale_ref[u] = jnp.dot(spread.astype(BF), pick_ref[...], preferred_element_type=F32)
        for u, xi in enumerate(xis):
            for y in range(8):
                x = step*xb + xi
                parts = []
                for kp in range(2):
                    r = jnp.where(left, load_at(idx_ref[y, 2*kp, x]), load_at(idx_ref[y, 2*kp+1, x]))
                    parts.append(jnp.where(even, r, zero))
                    parts.append(jnp.where(even, zero, r))
                rhs = jnp.concatenate(parts, axis=0)
                lhs = jnp.concatenate([abuf[slot, xi, y, 0], abuf[slot, xi, y, 1]], axis=1)
                wide[u, y] = jnp.dot(lhs, rhs, preferred_element_type=F32)
        for u, xi in enumerate(xis):
            for y in range(8):
                r = [[wide[u, y, pl.ds(32*ch+p, 16, stride=2), :] for p in range(2)] for ch in range(2)]
                v = jnp.where(lane < 64, r[0][0], r[1][1]) + pltpu.roll(jnp.where(lane < 64, r[1][0], r[0][1]), 64, 1)
                obuf[slot, xi, y] = t_ref[xi, y] - scale_ref[u, 16*y:16*y+16, :] * v
        return carry
    lax.fori_loop(0, xb//APPLY_UNROLL, some_rows, 0)
    for c in outs(step, slot): c.start()
    @pl.when(step == steps - 1)
    def _():
        for c in outs(step-1, 1-slot) + outs(step, slot): c.wait()


def apply_call(idx, t4, d, own, tp, a6, xb=12):
    nx = t4.shape[0]; px, py = tp.shape[:2]
    anyspec = pl.BlockSpec(memory_space=pl.ANY)
    return pl.pallas_call(functools.partial(apply_kernel, nx, px, py, xb),
        grid_spec=pltpu.PrefetchScalarGridSpec(num_scalar_prefetch=1, grid=(nx//xb,),
          in_specs=[pl.BlockSpec((xb,8,16,128), lambda i,*_:(i,0,0,0)), pl.BlockSpec((xb,8,64), lambda i,*_:(i,0,0)),
                    anyspec, anyspec, anyspec],
          out_specs=anyspec,
          scratch_shapes=[pltpu.VMEM((2,xb,8,2,64,128),BF), pltpu.VMEM((px,py,64,128),BF), pltpu.VMEM((APPLY_UNROLL,8,64,128),F32), pltpu.VMEM((12,64,128),F32), pltpu.VMEM((128,512),BF), pltpu.VMEM((128,128),BF), pltpu.VMEM((APPLY_UNROLL,128,128),F32),
             pltpu.VMEM((px,py,16,128),BF), pltpu.VMEM((2,xb,8,16,128),F32), pltpu.SemaphoreType.DMA((2,)), pltpu.SemaphoreType.DMA((2,8)), pltpu.SemaphoreType.DMA((5,))]),
        out_shape=jax.ShapeDtypeStruct((nx,16,8,128),F32),
        compiler_params=pltpu.CompilerParams(vmem_limit_bytes=62<<20), name="apply")(idx, t4, d, own, tp, a6)


def body(near_null, a_blocks, inv_diag, root_map, neighbours):
    nx, ny = root_map.shape
    grid_x, grid_y = nx * lax.axis_size("gx"), ny * lax.axis_size("gy")
    gx, gy = lax.axis_index("gx"), lax.axis_index("gy")
    sx, sy = gx * nx, gy * ny
    nn = near_null.reshape(nx, ny, 16, 128).transpose(0, 2, 1, 3)
    a5 = a_blocks.reshape(nx, ny, 4, 32, 128).transpose(0, 1, 3, 2, 4)
    roots = root_map.T
    gpad, glow, tiles = gram_call(nn, roots)
    around = tiles.transpose(0, 3, 1, 2).reshape(3 * nx, 3 * ny)[nx - 4:2 * nx + 4, ny - 4:2 * ny + 4]
    ax = sx - 4 + jnp.arange(nx + 8, dtype=jnp.int32)[:, None]
    ay = sy - 4 + jnp.arange(ny + 8, dtype=jnp.int32)[None, :]
    around = jnp.where((ax >= 0) & (ax < grid_x) & (ay >= 0) & (ay < grid_y), around, -1)
    cells = jnp.where(around == ax * grid_y + ay, around, -1)[2:-2, 2:-2].reshape(-1)
    rid = jnp.concatenate([around.reshape(nx + 8, 4, 4).transpose(1, 0, 2).reshape(1, -1), root_map.reshape(nx, 2, 4).transpose(1, 0, 2).reshape(1, -1)], axis=1)
    tent, low = factor_call(cells, roots, rid, nn, gpad.reshape(4, 8, -1, 128), glow.reshape(2, 8, -1, 128))
    low_pad, own_table = halo_call(low, (nx + 4, ny + 4, 16, 128), 2)
    out = apply_call(neighbours.transpose(1, 2, 0), tent, inv_diag, own_table, low_pad, a5)
    return out.transpose(0, 2, 1, 3).reshape(nx, ny, 2048)


def solution(mesh):
    in_specs = (P("gx", "gy", None), P("gx", "gy", None, None), P("gx", "gy", None), P("gx", "gy"), P("gx", "gy", None))
    return jax.shard_map(body, mesh=mesh, in_specs=in_specs, out_specs=P("gx", "gy", None), check_vma=False)
```

```python
import functools

import jax
import jax.numpy as jnp
from jax import lax
from jax.experimental import pallas as pl
from jax.experimental.pallas import tpu as pltpu
from jax.sharding import PartitionSpec as P

F32 = jnp.float32
BF = jnp.bfloat16
OMEGA = 2.0 / 3.0

SIDES = [(dx, dy) for dx in (-1, 0, 1) for dy in (-1, 0, 1) if dx or dy]


def there(dx, dy):
    gx, gy = lax.axis_index("gx"), lax.axis_index("gy")
    ok = jnp.bool_(True)
    if dx:
        ok &= (gx + dx >= 0) & (gx + dx < lax.axis_size("gx"))
    if dy:
        ok &= (gy + dy >= 0) & (gy + dy < lax.axis_size("gy"))
    return ok


def peer(dx, dy):
    return (lax.axis_index("gx") + dx, lax.axis_index("gy") + dy)


def remote(src, dst, send, recv, to):
    return pltpu.make_async_remote_copy(src_ref=src, dst_ref=dst, send_sem=send, recv_sem=recv, device_id=to, device_id_type=pl.DeviceIdType.MESH)


def greet():
    for dx, dy in SIDES:
        @pl.when(there(dx, dy))
        def _():
            pl.semaphore_signal(pltpu.get_barrier_semaphore(), inc=1, device_id=peer(dx, dy), device_id_type=pl.DeviceIdType.MESH)


def meet():
    gx, gy = lax.axis_index("gx"), lax.axis_index("gy")
    wide = 1 + (gx > 0).astype(jnp.int32) + (gx < lax.axis_size("gx") - 1).astype(jnp.int32)
    tall = 1 + (gy > 0).astype(jnp.int32) + (gy < lax.axis_size("gy") - 1).astype(jnp.int32)
    pl.semaphore_wait(pltpu.get_barrier_semaphore(), wide * tall - 1)


def send_all(messages, phase):
    for at, dx, dy, copy in messages:
        if at == phase:
            @pl.when(there(dx, dy))
            def _():
                copy(peer(dx, dy)).start()


def wait_all(messages):
    for _, dx, dy, copy in messages:
        @pl.when(there(-dx, -dy))
        def _():
            copy(peer(dx, dy)).wait_recv()
    for _, dx, dy, copy in messages:
        @pl.when(there(dx, dy))
        def _():
            copy(peer(dx, dy)).wait_send()


def spread_lanes():
    r = lax.broadcasted_iota(jnp.int32, (128, 512), 0)
    c = lax.broadcasted_iota(jnp.int32, (128, 512), 1)
    return jnp.where((r // 32 == c // 128) & (r % 32 == c % 32), 1.0, 0.0).astype(BF)


def expanded(rows, fan_ref, tall):
    o = jnp.dot(rows, fan_ref[...], preferred_element_type=F32)
    for e in range(rows.shape[0] // 16):
        for q in range(4):
            tall[e, pl.ds(q, 16, stride=4), :] = o[e*16:(e+1)*16, q*128:(q+1)*128]
    return [tall[e].astype(BF) for e in range(rows.shape[0] // 16)]


def halo_kernel(nx, ny, width, src, dst, own_table, buf, table, fan_ref, tall, load, store, send, recv):
    def taken(d, n):
        return {0: pl.ds(0, n), 1: pl.ds(n - width, width), -1: pl.ds(0, width)}[d]

    def landed(d, n):
        return {0: pl.ds(width, n), 1: pl.ds(0, width), -1: pl.ds(n + width, width)}[d]

    def message(s, dx, dy):
        return (0, dx, dy, lambda to: remote(src.at[taken(dx, nx), taken(dy, ny)], dst.at[landed(dx, nx), landed(dy, ny)], send.at[s], recv.at[s], to))

    messages = [message(s, dx, dy) for s, (dx, dy) in enumerate(SIDES)]
    greet()
    fill = pltpu.make_async_copy(src, buf, load.at[0])
    fill.start()
    fan_ref[...] = spread_lanes()
    meet()
    send_all(messages, 0)
    fill.wait()
    chunks = 4
    part = nx // chunks
    stores = []
    for c in range(chunks):
        def expand(i, carry):
            x = c*part + 3*i
            rows = jnp.concatenate([buf[x+u].reshape(ny*16, 128) for u in range(3)], axis=0)
            for e, t in enumerate(expanded(rows, fan_ref, tall)):
                table[x + e//ny, e % ny] = t
            return carry
        lax.fori_loop(0, part//3, expand, 0)
        xs = pl.ds(c*part, part)
        stores.append(pltpu.make_async_copy(table.at[xs], own_table.at[xs], store.at[c]))
        stores[-1].start()
    wait_all(messages)
    for s in stores:
        s.wait()


def halo_call(src, dst_shape, width):
    anyspec = pl.BlockSpec(memory_space=pl.ANY)
    nx, ny = src.shape[:2]
    return pl.pallas_call(functools.partial(halo_kernel, nx, ny, width),
        in_specs=[anyspec], out_specs=[anyspec]*2, out_shape=[jax.ShapeDtypeStruct(dst_shape, src.dtype), jax.ShapeDtypeStruct((nx, ny, 64, 128), BF)],
        scratch_shapes=[pltpu.VMEM(src.shape, BF), pltpu.VMEM((nx, ny, 64, 128), BF), pltpu.VMEM((128, 512), BF), pltpu.VMEM((3*ny, 64, 128), F32),
                        pltpu.SemaphoreType.DMA((1,)), pltpu.SemaphoreType.DMA((4,)), pltpu.SemaphoreType.DMA((8,)), pltpu.SemaphoreType.DMA((8,))],
        compiler_params=pltpu.CompilerParams(vmem_limit_bytes=62<<20, collective_id=1, has_side_effects=True), name="halo")(src)


UNROLL = 6


def pick_blocks(pieces, block):
    out = pieces[3]
    for b in (2, 1, 0):
        out = jnp.where(block == b, pieces[b], out)
    return out


def transpose_blocks(p, lane):
    block = lane >> 5
    return [pick_blocks([p[b] if b == q else pltpu.roll(p[b], 32*((b-q) % 4), 1) for b in range(4)], block) for q in range(4)]


def gram_rows(xs, p_buf, z_buf, g_buf, low_buf):
    lane16 = lax.broadcasted_iota(jnp.int32, (16,128), 1)
    lane8 = lax.broadcasted_iota(jnp.int32, (8,128), 1)
    block8 = lane8//32
    work = [(x, half) for x in xs for half in range(2)]
    outs = []
    for x, half in work:
        yh = jnp.concatenate(transpose_blocks([p_buf[x, 4*half+b] for b in range(4)], lane16), axis=0)
        hi = yh.astype(BF)
        lo = (yh - hi.astype(F32)).astype(BF)
        outs.append(lax.dot_general(jnp.concatenate([hi, lo, hi], axis=0), jnp.concatenate([hi, hi, lo], axis=0), (((0,),(0,)),((),())), preferred_element_type=F32))
    for slot, o in enumerate(outs):
        r = [pick_blocks([o[32*b+8*kb:32*b+8*kb+8] for b in range(4)], block8) * (1.0/64) for kb in range(4)]
        for b, g in enumerate(transpose_blocks(r, lane8)):
            z_buf[slot, pl.ds(b, 8, stride=4), :] = g
    for slot, (x, half) in enumerate(work):
        z = z_buf[slot]
        zh = z.astype(BF)
        g_buf[half, :, x] = zh.reshape(8,4,128)
        low_buf[half, :, x] = (z - zh.astype(F32)).astype(BF).reshape(8,4,128)


def gram_kernel(nx, chunks, with_halo, *refs):
    if with_halo:
        b_ref, tile, gpad, glow, tiles, p_buf, z_buf, g_buf, low_buf, load, store, send, recv = refs
    else:
        b_ref, gpad, glow, p_buf, z_buf, g_buf, low_buf, load, store = refs
    part = nx // chunks
    loads = [[pltpu.make_async_copy(b_ref.at[pl.ds(c*part, part), :, y], p_buf.at[pl.ds(c*part, part), y], load.at[c, y]) for y in range(8)] for c in range(chunks)]
    for group in loads:
        for c in group: c.start()
    messages = []
    if with_halo:
        def block(phase, dx, dy, sx, tx):
            sy = {0: pl.ds(0, 2), 1: pl.ds(1, 1), -1: pl.ds(0, 1)}[dy]
            ty = {0: pl.ds(1, 2), 1: pl.ds(0, 1), -1: pl.ds(3, 1)}[dy]
            s = len(messages)
            messages.append((phase, dx, dy, lambda to: remote(g_buf.at[sy, :, sx], gpad.at[ty, :, tx], send.at[s], recv.at[s], to)))
        def roots(dx, dy):
            s = len(messages)
            messages.append((0, dx, dy, lambda to: remote(tile, tiles.at[1-dx, 1-dy], send.at[s], recv.at[s], to)))
        for dx, dy in SIDES:
            roots(dx, dy)
        for dy in (-1, 0, 1):
            block(0, -1, dy, pl.ds(0, 4), pl.ds(nx+4, 4))
            block(chunks-1, 1, dy, pl.ds(nx-4, 4), pl.ds(0, 4))
        for c in range(chunks):
            for dy in (-1, 1):
                block(c, 0, dy, pl.ds(c*part, part), pl.ds(4 + c*part, part))
        greet()
    for c in range(chunks):
        for one in loads[c]: one.wait()
        def rows(i, carry):
            gram_rows([c*part + UNROLL*i + u for u in range(UNROLL)], p_buf, z_buf, g_buf, low_buf)
            return carry
        lax.fori_loop(0, part//UNROLL, rows, 0)
        if with_halo:
            if c == 0:
                meet()
            send_all(messages, c)
    mine = [pltpu.make_async_copy(g_buf, gpad.at[pl.ds(1, 2), :, pl.ds(4, nx)], store.at[0]), pltpu.make_async_copy(low_buf, glow, store.at[1])]
    if with_halo:
        mine.append(pltpu.make_async_copy(tile, tiles.at[1, 1], store.at[2]))
    for c in mine: c.start()
    if with_halo:
        wait_all(messages)
    for c in mine: c.wait()


def gram_call(nn, tile=None, chunks=4):
    nx = nn.shape[0]
    anyspec = pl.BlockSpec(memory_space=pl.ANY)
    gshape = jax.ShapeDtypeStruct((4, 8, nx+8, 4, 128), BF)
    scratch = [pltpu.VMEM((nx,8,16,128),F32), pltpu.VMEM((2*UNROLL,32,128),F32), pltpu.VMEM((2,8,nx,4,128),BF), pltpu.VMEM((2,8,nx,4,128),BF),
               pltpu.SemaphoreType.DMA((chunks,8)), pltpu.SemaphoreType.DMA((3,))]
    lshape = jax.ShapeDtypeStruct((2, 8, nx, 4, 128), BF)
    kern = functools.partial(gram_kernel, nx, chunks, tile is not None)
    if tile is None:
        return pl.pallas_call(kern, in_specs=[anyspec], out_specs=[anyspec]*2, out_shape=[gshape, lshape], scratch_shapes=scratch,
            compiler_params=pltpu.CompilerParams(vmem_limit_bytes=62<<20), name="gram")(nn)
    return pl.pallas_call(kern, in_specs=[anyspec]*2, out_specs=[anyspec]*3,
        out_shape=[gshape, lshape, jax.ShapeDtypeStruct((3,3)+tile.shape, tile.dtype)],
        scratch_shapes=scratch + [pltpu.SemaphoreType.DMA((14 + 2*chunks,)), pltpu.SemaphoreType.DMA((14 + 2*chunks,))],
        compiler_params=pltpu.CompilerParams(vmem_limit_bytes=62<<20, collective_id=0, has_side_effects=True), name="gram")(nn, tile)


FACTOR_UNROLL = 4


def local_slots(nx, ny):
    grid_y = ny * lax.axis_size("gy")
    first_x, first_y = lax.axis_index("gx")*nx - 2, lax.axis_index("gy")*ny - 2
    bits = grid_y.bit_length() - 1

    def place(flat):
        x = lax.shift_right_logical(flat, bits) if grid_y == 1 << bits else lax.div(flat, grid_y)
        return x - first_x, flat - x*grid_y - first_y
    return place


def factor_kernel(nx, cells_ref, root_ref, rid_ref, b_ref, g_ref, gl_ref, t_ref, tb_ref, comp, idcol, tab, bd, v_ref, g_buf, gl_buf, p_buf, t_buf, tb_buf, sem, load, store):
    ncell = cells_ref.shape[0]
    px = nx + 8
    gx, gy = lax.axis_index("gx"), lax.axis_index("gy")
    place = local_slots(nx, 8)
    els = rid_ref.shape[1]
    chunks = 4
    part = nx // chunks
    copies_g = [pltpu.make_async_copy(g_ref, g_buf, sem.at[0]), pltpu.make_async_copy(gl_ref, gl_buf, sem.at[1])]
    for c in copies_g: c.start()
    loads = [pltpu.make_async_copy(b_ref.at[:, :, y], p_buf.at[:, y], load.at[y]) for y in range(8)]
    for c in loads: c.start()
    def compact(i, n):
        cid = cells_ref[i]
        idcol[pl.ds(n, 1), :] = jnp.full((1, 128), cid, jnp.int32)
        comp[i] = n
        return n + (cid >= 0).astype(jnp.int32)
    n = lax.fori_loop(0, ncell, compact, 0, unroll=8)
    for c in copies_g: c.wait()
    @pl.when(gx == 0)
    def _(): g_buf[:, :, 0:16] = jnp.zeros((4, 8, 16, 128), BF)
    @pl.when(gx == lax.axis_size("gx") - 1)
    def _(): g_buf[:, :, 4*px-16:4*px] = jnp.zeros((4, 8, 16, 128), BF)
    @pl.when(gy == 0)
    def _(): g_buf[0] = jnp.zeros((8, 4*px, 128), BF)
    @pl.when(gy == lax.axis_size("gy") - 1)
    def _(): g_buf[3] = jnp.zeros((8, 4*px, 128), BF)

    sub = lax.broadcasted_iota(jnp.int32, (32, 128), 0)
    block = lax.broadcasted_iota(jnp.int32, (32, 128), 1)//32
    def batch(bi, c):
        base = bi*128
        ids = idcol[pl.ds(base, 128), :]
        hot = [jnp.where(ids == rid_ref[:, 128*t:128*t+128], 1.0, 0.0).astype(BF) for t in range(els//128)]
        hot = jnp.concatenate(hot, axis=1)
        for k8 in range(8):
            g = jnp.concatenate([g_buf[yb, k8] for yb in range(4)] + [gl_buf[yb, k8] for yb in range(2)], axis=0)
            s = jnp.dot(hot, g, preferred_element_type=F32).T
            for kb in range(4):
                v_ref[32*(8*kb+k8):32*(8*kb+k8)+32, :] = s[32*kb:32*kb+32]
        for jb in range(4):
            def pivot(j8, c2):
                j = jb*8 + j8
                row = v_ref[pl.ds(pl.multiple_of(j*32, 32), 32), :]
                d = lax.rsqrt(v_ref[pl.ds(j*33, 1), :])
                at_j = sub == j
                u = jnp.where(at_j, d, row*d)
                v_ref[pl.ds(pl.multiple_of(j*32, 32), 32), :] = u
                for i in range(jb*8, 32):
                    f = u[i:i+1, :]
                    old = v_ref[32*i:32*i+32, :]
                    if i < jb*8+8:
                        later = i > j
                        f = jnp.where(later, f, 0.0)
                        new = jnp.where(at_j & later, 0.0, old) - f*u
                        new = jnp.where(later, new, old)
                    else:
                        new = jnp.where(at_j, 0.0, old) - f*u
                    v_ref[32*i:32*i+32, :] = new
                return c2
            lax.fori_loop(0, 8, pivot, 0)
        for k in range(32):
            m = v_ref[pl.ds(k, 32, stride=32), :]
            m = jnp.where(sub >= k, m, 0.0)
            tab[k] = jnp.concatenate([m]*4, axis=0).T
        def spread(i, c2):
            for u in range(4):
                r = 4*i + u
                w = tab[:, pl.ds(r, 1), :].reshape(32, 128)
                hi = w.astype(BF).astype(F32)
                lo = w - hi
                bd[base + r, 0:128, :] = jnp.concatenate([jnp.where(block == q, hi, 0.0) for q in range(4)], axis=0).astype(BF)
                bd[base + r, 128:256, :] = jnp.concatenate([jnp.where(block == q, lo, 0.0) for q in range(4)], axis=0).astype(BF)
            return c2
        lax.fori_loop(0, (jnp.minimum(n - base, 128) + 3)//4, spread, 0)
        return c
    lax.fori_loop(0, (n + 127)//128, batch, 0)

    for c in loads: c.wait()
    stores = []
    for ch in range(chunks):
        def rows(i, c):
            at = [(ch*part + FACTOR_UNROLL*i + u, y) for u in range(FACTOR_UNROLL) for y in range(8)]
            outs = []
            for x, y in at:
                rx, ry = place(root_ref[y, x])
                r = comp[rx*12 + ry]
                p = p_buf[x, y]
                ph = p.astype(BF)
                plo = (p - ph.astype(F32)).astype(BF)
                lhs = jnp.concatenate([jnp.concatenate([ph, ph], axis=1), jnp.concatenate([plo, jnp.zeros_like(plo)], axis=1)], axis=0)
                outs.append(jnp.dot(lhs, bd[r], preferred_element_type=F32))
            for (x, y), o in zip(at, outs):
                t = o[:16] + o[16:]
                t_buf[x, y] = t
                tb_buf[x, y] = t.astype(BF)
            return c
        lax.fori_loop(0, part//FACTOR_UNROLL, rows, 0)
        xs = pl.ds(ch*part, part)
        for c in (pltpu.make_async_copy(t_buf.at[xs], t_ref.at[xs], store.at[0, ch]), pltpu.make_async_copy(tb_buf.at[xs], tb_ref.at[xs], store.at[1, ch])):
            c.start()
            stores.append(c)
    for c in stores: c.wait()


def factor_call(cells, roots, rid, nn, gpad, glow):
    nx = nn.shape[0]
    anyspec = pl.BlockSpec(memory_space=pl.ANY)
    nc = (nx+4)*12
    ncp = (nc + 127)//128*128
    return pl.pallas_call(functools.partial(factor_kernel, nx),
        grid_spec=pltpu.PrefetchScalarGridSpec(num_scalar_prefetch=2, grid=(1,),
          in_specs=[pl.BlockSpec(rid.shape, lambda i,*_: (0,0)), anyspec, anyspec, anyspec],
          out_specs=[anyspec, anyspec],
          scratch_shapes=[pltpu.SMEM((nc,), jnp.int32), pltpu.VMEM((ncp+128,128), jnp.int32), pltpu.VMEM((32,128,128),F32), pltpu.VMEM((ncp,256,128),BF),
             pltpu.VMEM((1024,128),F32), pltpu.VMEM(gpad.shape,BF), pltpu.VMEM(glow.shape,BF), pltpu.VMEM((nx,8,16,128),F32), pltpu.VMEM((nx,8,16,128),F32), pltpu.VMEM((nx,8,16,128),BF),
             pltpu.SemaphoreType.DMA((2,)), pltpu.SemaphoreType.DMA((8,)), pltpu.SemaphoreType.DMA((2,4))]),
        out_shape=[jax.ShapeDtypeStruct((nx,8,16,128),F32), jax.ShapeDtypeStruct((nx,8,16,128),BF)],
        compiler_params=pltpu.CompilerParams(vmem_limit_bytes=62<<20), name="factor")(cells, roots, rid, nn, gpad, glow)


APPLY_UNROLL = 6


def apply_kernel(nx, px, py, xb, idx_ref, t_ref, d_ref, own_ref, tp_ref, a_ref, out_ref, abuf, table, wide, tall, fan_ref, pick_ref, scale_ref, tbuf, obuf, sems, osem, tsem):
    step = pl.program_id(0)
    steps = nx // xb
    slot = lax.rem(step, 2)
    def fetch(s, slot):
        for c in range(32):
            for kp in range(2):
                pltpu.make_async_copy(a_ref.at[pl.ds(s*xb, xb), :, c, pl.ds(2*kp, 2), :], abuf.at[slot, :, :, kp, pl.ds(32*(c % 2) + 2*(c//2), 2), :], sems.at[slot]).start()
    def outs(s, slot):
        return [pltpu.make_async_copy(obuf.at[slot, :, y], out_ref.at[pl.ds(s*xb, xb), :, y], osem.at[slot, y]) for y in range(8)]
    lane = lax.broadcasted_iota(jnp.int32, (16, 128), 1)
    place = local_slots(nx, 8)
    def load_at(flat):
        tx, ty = place(flat)
        return table[tx, ty]
    @pl.when(step == 0)
    def _():
        strips = [(pl.ds(0, 2), pl.ds(0, py)), (pl.ds(px-2, 2), pl.ds(0, py)), (pl.ds(2, nx), pl.ds(0, 2)), (pl.ds(2, nx), pl.ds(py-2, 2))]
        fill = [pltpu.make_async_copy(tp_ref.at[sx, sy], tbuf.at[sx, sy], tsem.at[i]) for i, (sx, sy) in enumerate(strips)]
        own = pltpu.make_async_copy(own_ref, table.at[pl.ds(2, nx), pl.ds(2, py-4)], tsem.at[4])
        for c in fill: c.start()
        own.start()
        fetch(0, 0)
        fan_ref[...] = spread_lanes()
        pick_ref[...] = jnp.where((lax.broadcasted_iota(jnp.int32, (128, 128), 0) & 3) == lax.broadcasted_iota(jnp.int32, (128, 128), 1) >> 5, 1.0, 0.0).astype(BF)
        for c in fill: c.wait()
        def ends(i, carry):
            x = i*(px - 2)
            rows = jnp.concatenate([tbuf[x+u].reshape(py*16, 128) for u in range(2)], axis=0)
            for e, t in enumerate(expanded(rows, fan_ref, tall)):
                table[x + e//py, e % py] = t
            return carry
        lax.fori_loop(0, 2, ends, 0)
        def sides(i, carry):
            at = [(2 + 6*i + u, y) for u in range(6) for y in (0, 1, py-2, py-1)]
            rows = jnp.concatenate([tbuf[x, y] for x, y in at], axis=0)
            for (x, y), t in zip(at, expanded(rows, fan_ref, tall)):
                table[x, y] = t
            return carry
        lax.fori_loop(0, nx//6, sides, 0)
        own.wait()
    @pl.when(step + 1 < steps)
    def _():
        fetch(step+1, 1-slot)
    @pl.when(step >= 2)
    def _():
        for c in outs(step-2, slot): c.wait()
    pltpu.make_async_copy(abuf.at[slot], abuf.at[slot], sems.at[slot]).wait()
    diagonal = (lax.broadcasted_iota(jnp.int32, (16, 128), 1) & 63) >> 2 == lax.broadcasted_iota(jnp.int32, (16, 128), 0)
    lanew = lax.broadcasted_iota(jnp.int32, (64, 128), 1)
    even = (lanew & 32) == 0
    left = lanew < 64
    zero = jnp.zeros((64, 128), BF)
    def some_rows(i, carry):
        xis = [APPLY_UNROLL*i + u for u in range(APPLY_UNROLL)]
        for u, xi in enumerate(xis):
            d = d_ref[xi] * OMEGA
            hi = d.astype(BF).astype(F32)
            both = jnp.concatenate([hi, d - hi], axis=1)
            spread = jnp.concatenate([jnp.where(diagonal, both[y:y+1], 0.0) for y in range(8)], axis=0)
            scale_ref[u] = jnp.dot(spread.astype(BF), pick_ref[...], preferred_element_type=F32)
        for u, xi in enumerate(xis):
            for y in range(8):
                x = step*xb + xi
                parts = []
                for kp in range(2):
                    r = jnp.where(left, load_at(idx_ref[y, 2*kp, x]), load_at(idx_ref[y, 2*kp+1, x]))
                    parts.append(jnp.where(even, r, zero))
                    parts.append(jnp.where(even, zero, r))
                rhs = jnp.concatenate(parts, axis=0)
                lhs = jnp.concatenate([abuf[slot, xi, y, 0], abuf[slot, xi, y, 1]], axis=1)
                wide[u, y] = jnp.dot(lhs, rhs, preferred_element_type=F32)
        for u, xi in enumerate(xis):
            for y in range(8):
                r = [[wide[u, y, pl.ds(32*ch+p, 16, stride=2), :] for p in range(2)] for ch in range(2)]
                v = jnp.where(lane < 64, r[0][0], r[1][1]) + pltpu.roll(jnp.where(lane < 64, r[1][0], r[0][1]), 64, 1)
                obuf[slot, xi, y] = t_ref[xi, y] - scale_ref[u, 16*y:16*y+16, :] * v
        return carry
    lax.fori_loop(0, xb//APPLY_UNROLL, some_rows, 0)
    for c in outs(step, slot): c.start()
    @pl.when(step == steps - 1)
    def _():
        for c in outs(step-1, 1-slot) + outs(step, slot): c.wait()


def apply_call(idx, t4, d, own, tp, a6, xb=12):
    nx = t4.shape[0]; px, py = tp.shape[:2]
    anyspec = pl.BlockSpec(memory_space=pl.ANY)
    return pl.pallas_call(functools.partial(apply_kernel, nx, px, py, xb),
        grid_spec=pltpu.PrefetchScalarGridSpec(num_scalar_prefetch=1, grid=(nx//xb,),
          in_specs=[pl.BlockSpec((xb,8,16,128), lambda i,*_:(i,0,0,0)), pl.BlockSpec((xb,8,64), lambda i,*_:(i,0,0)),
                    anyspec, anyspec, anyspec],
          out_specs=anyspec,
          scratch_shapes=[pltpu.VMEM((2,xb,8,2,64,128),BF), pltpu.VMEM((px,py,64,128),BF), pltpu.VMEM((APPLY_UNROLL,8,64,128),F32), pltpu.VMEM((24,64,128),F32), pltpu.VMEM((128,512),BF), pltpu.VMEM((128,128),BF), pltpu.VMEM((APPLY_UNROLL,128,128),F32),
             pltpu.VMEM((px,py,16,128),BF), pltpu.VMEM((2,xb,8,16,128),F32), pltpu.SemaphoreType.DMA((2,)), pltpu.SemaphoreType.DMA((2,8)), pltpu.SemaphoreType.DMA((5,))]),
        out_shape=jax.ShapeDtypeStruct((nx,16,8,128),F32),
        compiler_params=pltpu.CompilerParams(vmem_limit_bytes=62<<20), name="apply")(idx, t4, d, own, tp, a6)


def body(near_null, a_blocks, inv_diag, root_map, neighbours):
    nx, ny = root_map.shape
    grid_x, grid_y = nx * lax.axis_size("gx"), ny * lax.axis_size("gy")
    gx, gy = lax.axis_index("gx"), lax.axis_index("gy")
    sx, sy = gx * nx, gy * ny
    nn = near_null.reshape(nx, ny, 16, 128).transpose(0, 2, 1, 3)
    a5 = a_blocks.reshape(nx, ny, 4, 32, 128).transpose(0, 1, 3, 2, 4)
    roots = root_map.T
    gpad, glow, tiles = gram_call(nn, roots)
    around = tiles.transpose(0, 3, 1, 2).reshape(3 * nx, 3 * ny)[nx - 4:2 * nx + 4, ny - 4:2 * ny + 4]
    ax = sx - 4 + jnp.arange(nx + 8, dtype=jnp.int32)[:, None]
    ay = sy - 4 + jnp.arange(ny + 8, dtype=jnp.int32)[None, :]
    around = jnp.where((ax >= 0) & (ax < grid_x) & (ay >= 0) & (ay < grid_y), around, -1)
    cells = jnp.where(around == ax * grid_y + ay, around, -1)[2:-2, 2:-2].reshape(-1)
    rid = jnp.concatenate([around.reshape(nx + 8, 4, 4).transpose(1, 0, 2).reshape(1, -1), root_map.reshape(nx, 2, 4).transpose(1, 0, 2).reshape(1, -1)], axis=1)
    tent, low = factor_call(cells, roots, rid, nn, gpad.reshape(4, 8, -1, 128), glow.reshape(2, 8, -1, 128))
    low_pad, own_table = halo_call(low, (nx + 4, ny + 4, 16, 128), 2)
    out = apply_call(neighbours.transpose(1, 2, 0), tent, inv_diag, own_table, low_pad, a5)
    return out.transpose(0, 2, 1, 3).reshape(nx, ny, 2048)


def solution(mesh):
    in_specs = (P("gx", "gy", None), P("gx", "gy", None, None), P("gx", "gy", None), P("gx", "gy"), P("gx", "gy", None))
    return jax.shard_map(body, mesh=mesh, in_specs=in_specs, out_specs=P("gx", "gy", None), check_vma=False)
```
